32 devices in a mesh: context: 8 (over z, core), expert: 4 (over y, x).
Axes of the slice: x: 2, y: 2, z: 4, core: 2. Of those that a mesh axis runs over, the one named last changes fastest.
Arguments:
- residual: bfloat16 [2048, 6144], P(('context', 'expert')), may hold values from -6 to 6
- attn_queries: bfloat16 [2048, 8192], P('context', 'expert'), may hold values from -6 to 6
- attn_keys: bfloat16 [2048, 8192], P('context', 'expert'), may hold values from -0.5 to 0.5
- attn_values: bfloat16 [2048, 8192], P('context', 'expert'), may hold values from -6 to 6
- decay_rate: float32 [64, 2048], P('expert', 'context'), may hold values from 0 to 1, as said below
- start_state: float32 [64, 128, 128], P('expert'), may hold values from -12 to 12
- out_proj: bfloat16 [8192, 6144], P('expert', 'context'), may hold values from -0.0625 to 0.0625
- moe_gain: float32 [6144], replicated, may hold values from 0.5 to 1.5
- gate_proj: bfloat16 [4, 6144, 4608], P('expert', None, 'context'), may hold values from -0.078125 to 0.078125
- up_proj: bfloat16 [4, 6144, 4608], P('expert', None, 'context'), may hold values from -0.078125 to 0.078125
- down_proj: bfloat16 [4, 4608, 6144], P('expert', None, 'context'), may hold values from -0.09375 to 0.09375
- expert_ids: int32 [2048, 2], P(('context', 'expert')), may hold values from 0 to 3, all different within a row; in each aligned block of 64 rows (0 to 63, 64 to 127, ...) at most 48 rows name the same one
- expert_gates: float32 [2048, 2], P(('context', 'expert')), may hold values from 0.25 to 1
Outputs:
- layer_out: bfloat16 [2048, 6144], P(('context', 'expert'))
The draws below stay inside these ranges and needn't reach their ends.
Inputs may be any that keep to these rules, and one draw needn't show every extreme that they name: `decay_rate`: non-negative rates. `expert_ids`: each row names two different experts; among the 64 rows of one aligned block no expert is named by more than 48 rows.
All inputs are finite; a program needn't handle non-finite values.
Results may differ from the reference program's by a relative error of at most 0.015.
Values may be sent and summed in bfloat16 or wider, within the bound.
No kernel may reach another device: no remote copies, remote signals or barrier semaphores. Data moves between devices by JAX's collectives and lax.ppermute only.
A program may use at most 192 MiB of HBM per device.

```python
import math
import jax
import jax.numpy as jnp
import numpy as np
from jax import lax

D = 6144
ATTENTION_PARTS = 64
HD = 128
FF = 4608
TOK_DEV = 256
PROMPT_POSITIONS = 2048
HEADS_DEV = 16
MOE_DEV = 64
EXPERTS = 4
CAP = 48
N_CONTEXT = 8
N_EXPERT = 4


def draw_decay_rate(key, part):
    lookup_vectors = jax.random.split(jax.random.fold_in(key, 11), 6)
    fast_share = 0.5
    fast = jax.random.uniform(lookup_vectors[0], (ATTENTION_PARTS,), jnp.float32) < fast_share
    slow_base = jnp.exp(jax.random.uniform(lookup_vectors[1], (ATTENTION_PARTS,), jnp.float32, jnp.log(0.1), jnp.log(0.8))) / PROMPT_POSITIONS
    fast_base = jnp.exp(jax.random.uniform(lookup_vectors[2], (ATTENTION_PARTS,), jnp.float32, jnp.log(1.0 / 50.0), jnp.log(1.0 / 30.0)))
    starting_shift = jnp.where(fast, fast_base, slow_base)
    approximate_guess = jax.random.uniform(lookup_vectors[3], (ATTENTION_PARTS, PROMPT_POSITIONS), jnp.float32, 0.5, 1.5)
    specialist_usage_tally = jax.random.randint(lookup_vectors[4], (ATTENTION_PARTS, PROMPT_POSITIONS), 0, PROMPT_POSITIONS // 2) == 0
    window_span = jnp.where(specialist_usage_tally, jax.random.uniform(lookup_vectors[5], (ATTENTION_PARTS, PROMPT_POSITIONS), jnp.float32, 0.22, 0.69), 0.0)
    return (starting_shift[:, None] * approximate_guess + window_span).astype(jnp.float32)


def level_of(stream_key, dims, cuts, least, high):
    level, own = 1.0, jax.random.fold_in(stream_key, 6)
    for dim, shards_of in cuts:
        draws = jnp.exp(jax.random.uniform(jax.random.fold_in(own, dim), (shards_of,), jnp.float32, least / len(cuts), high / len(cuts)))
        level = level * jnp.repeat(draws, dims[dim] // shards_of).reshape([-1 if axis == dim else 1 for axis in range(len(dims))])
    return level


def assign_block(rng, own, number, rows, amount, top, bound, skew):
    ranking = jax.random.permutation(rng, amount)
    packed, common = load_shares(amount, rows * top, bound, skew, True), load_shares(amount, rows * top, bound, skew, False)
    places = jnp.arange(amount)

    def named(sizes, offset_by):
        used = int((sizes > 0).sum())
        fixed = max(1, used // 4)
        passed = fixed + (places - fixed + offset_by * (used - fixed)) % max(1, amount - fixed)
        return jnp.zeros((amount,), jnp.int32).at[ranking[jnp.where(places < fixed, places, passed)]].set(jnp.asarray(sizes, jnp.int32))

    sizes = jnp.where(number % 4 == 0, named(packed, number // 4), named(common, number - number // 4 - 1))
    mixed = jax.random.permutation(jax.random.fold_in(own, 3), amount)
    giver, receiver = mixed[0:amount // 2 * 2:2], mixed[1:amount // 2 * 2:2]
    margin = jnp.minimum(sizes[giver] - 1, bound - sizes[receiver]) // 2
    margin = jnp.where((giver == ranking[0]) | (receiver == ranking[0]) | (sizes[receiver] == 0), 0, jnp.maximum(margin, 0))
    passed = jax.random.randint(jax.random.fold_in(own, 4), (amount // 2,), 0, 1 << 20) % (margin + 1)
    sizes = sizes.at[giver].add(-passed).at[receiver].add(passed)
    members = jnp.searchsorted(jnp.cumsum(sizes), jnp.arange(rows * top), side="right").astype(jnp.int32)
    listing = members.reshape(top, rows).T
    listing = listing[jax.random.permutation(jax.random.fold_in(own, 1), rows)]
    offset_by = jax.random.randint(jax.random.fold_in(own, 2), (rows, 1), 0, top)
    return jnp.take_along_axis(listing, (jnp.arange(top)[None, :] + offset_by) % top, axis=1)


def load_shares(number_of, total, most, skew, full):
    portions = [(1 << 20) // math.isqrt(rank ** skew) + 1 for rank in range(1, number_of + 1)]
    largest = most if full else min(most, max(-(-total // number_of), total * portions[0] // sum(portions)))
    least = 1 if total - largest >= number_of - 1 else 0
    given, rest = [largest] + [least] * (number_of - 1), total - largest - least * (number_of - 1)
    while rest > 0:
        candidates = [i for i in range(1, number_of) if given[i] < largest] or [i for i in range(1, number_of) if given[i] < most]
        whole, budget = sum([portions[i] for i in candidates]), rest
        for i in candidates:
            more = min(most - given[i], max(1, budget * portions[i] // whole), rest)
            given[i] = given[i] + more
            rest = rest - more
    return np.array(given)


def centred(stream_key, dims, scale, most, pieces=(), kind=jnp.bfloat16):
    values = scale * jax.random.normal(stream_key, dims, jnp.float32)
    if pieces:
        values = values * level_of(stream_key, dims, pieces, -0.22, 0.18)
    return jnp.clip(values, -most, most).astype(kind)


def setup_inputs(seed: int = 0) -> dict:
    streams_of = jax.random.split(jax.random.key(seed), 14)
    residual = centred(streams_of[0], (PROMPT_POSITIONS, D), 1.0, 6.0, ((0, 32),))
    attn_queries = centred(streams_of[1], (PROMPT_POSITIONS, ATTENTION_PARTS * HD), 1.0, 6.0, ((0, 8), (1, 4)))
    attn_keys = centred(streams_of[2], (PROMPT_POSITIONS, ATTENTION_PARTS * HD), HD ** -0.5, 0.5, ((0, 8), (1, 4)))
    attn_values = centred(streams_of[3], (PROMPT_POSITIONS, ATTENTION_PARTS * HD), 1.0, 6.0, ((0, 8), (1, 4)))
    decay_rate = draw_decay_rate(jax.random.fold_in(streams_of[13], 71), 0)
    start_state = centred(streams_of[5], (ATTENTION_PARTS, HD, HD), 2.0, 12.0, ((0, 4),), jnp.float32)
    out_proj = centred(streams_of[6], (ATTENTION_PARTS * HD, D), (ATTENTION_PARTS * HD) ** -0.5, 0.0625, ((0, 4), (1, 8)))
    moe_gain = jnp.clip(1.0 + 0.1 * jax.random.normal(streams_of[7], (D,), jnp.float32), 0.5, 1.5)
    gate_proj = centred(streams_of[8], (EXPERTS, D, FF), D ** -0.5, 0.078125, ((0, 4), (2, 8)))
    up_proj = centred(streams_of[9], (EXPERTS, D, FF), D ** -0.5, 0.078125, ((0, 4), (2, 8)))
    down_proj = centred(streams_of[10], (EXPERTS, FF, D), FF ** -0.5, 0.09375, ((0, 4), (2, 8)))
    expert_ids_keys = jax.random.split(jax.random.fold_in(streams_of[11], 1), PROMPT_POSITIONS // MOE_DEV)
    expert_ids_turns = jax.random.permutation(jax.random.fold_in(streams_of[11], 3), PROMPT_POSITIONS // MOE_DEV)
    expert_ids = jax.vmap(lambda own, number: assign_block(jax.random.fold_in(streams_of[11], 2), own, number, MOE_DEV, EXPERTS, 2, CAP, 2))(expert_ids_keys, expert_ids_turns).reshape((PROMPT_POSITIONS, 2))
    expert_gates = jnp.clip(0.25 + 0.75 * jax.random.uniform(streams_of[12], (PROMPT_POSITIONS, 2), jnp.float32) ** level_of(streams_of[12], (PROMPT_POSITIONS, 2), ((0, 32),), -0.2, 0.2), 0.25, 1.0)
    return dict(residual=residual, attn_queries=attn_queries, attn_keys=attn_keys, attn_values=attn_values, decay_rate=decay_rate, start_state=start_state, out_proj=out_proj, moe_gain=moe_gain, gate_proj=gate_proj, up_proj=up_proj, down_proj=down_proj, expert_ids=expert_ids, expert_gates=expert_gates)


def stretch_step(state, inputs):
    queries, keys_in, values_in, rates = inputs
    cum = jnp.cumsum(rates, axis=1)
    total = cum[:, -1]
    length = queries.shape[0]
    positions = jnp.arange(length)
    causal = (positions[None, :] <= positions[:, None])[None, :, :]
    diff = cum[:, None, :] - cum[:, :, None]
    decay = jnp.where(causal, jnp.exp(jnp.where(causal, diff, 0.0)), 0.0)
    q32 = queries.astype(jnp.float32)
    k32 = keys_in.astype(jnp.float32)
    v32 = values_in.astype(jnp.float32)
    scores = jnp.einsum('thd,shd->hts', q32, k32)
    weights = (scores * decay).astype(jnp.bfloat16)
    intra = jnp.einsum('hts,shd->thd', weights.astype(jnp.float32), v32)
    inter = jnp.einsum('thd,hde->the', q32, state, precision=lax.Precision.HIGHEST)
    inter = inter * jnp.exp(-cum).T[:, :, None]
    scaled_keys = k32 * jnp.exp(cum - total[:, None]).T[:, :, None]
    local = jnp.einsum('shd,she->hde', scaled_keys, v32, precision=lax.Precision.HIGHEST)
    new_state = jnp.exp(-total)[:, None, None] * state + local
    return (new_state, intra + inter)

def reference(residual, attn_queries, attn_keys, attn_values, decay_rate, start_state, out_proj, moe_gain, gate_proj, up_proj, down_proj, expert_ids, expert_gates):
    shaped_q = attn_queries.reshape(N_CONTEXT, TOK_DEV, ATTENTION_PARTS, HD)
    shaped_k = attn_keys.reshape(N_CONTEXT, TOK_DEV, ATTENTION_PARTS, HD)
    shaped_v = attn_values.reshape(N_CONTEXT, TOK_DEV, ATTENTION_PARTS, HD)
    shaped_g = decay_rate.reshape(ATTENTION_PARTS, N_CONTEXT, TOK_DEV).transpose(1, 0, 2)
    final_state, attended = lax.scan(stretch_step, start_state, (shaped_q, shaped_k, shaped_v, shaped_g))
    attended = attended.reshape(PROMPT_POSITIONS, ATTENTION_PARTS, HD)
    scale = lax.rsqrt(lax.optimization_barrier(jnp.mean(attended * attended, axis=-1, keepdims=True)) + 1e-06)
    head_out = (attended * scale).astype(jnp.bfloat16).reshape(PROMPT_POSITIONS, ATTENTION_PARTS * HD)
    width = HEADS_DEV * HD
    grouped = head_out.reshape(PROMPT_POSITIONS, N_EXPERT, width)

    def group_step(total, group):
        columns = lax.dynamic_index_in_dim(grouped, group, 1, keepdims=False)
        rows = lax.dynamic_slice_in_dim(out_proj, group * width, width, 0)
        part = jnp.dot(columns, rows, preferred_element_type=jnp.float32)
        rounded = lax.optimization_barrier(part.astype(jnp.bfloat16))
        return (total + rounded.astype(jnp.float32), None)
    projected, unused = lax.scan(group_step, jnp.zeros((PROMPT_POSITIONS, D), jnp.float32), jnp.arange(N_EXPERT, dtype=jnp.int32))
    stream = (residual.astype(jnp.float32) + projected).astype(jnp.bfloat16)
    stream32 = stream.astype(jnp.float32)
    moe_in = (stream32 * lax.rsqrt(lax.optimization_barrier(jnp.mean(stream32 * stream32, axis=-1, keepdims=True)) + 1e-06) * moe_gain).astype(jnp.bfloat16)
    flat_ids = expert_ids.reshape(-1)
    flat_gates = expert_gates.reshape(-1)
    most_rows = N_CONTEXT * N_EXPERT * CAP

    def expert_step(total, expert):
        chosen = flat_ids == expert
        index = jnp.nonzero(chosen, size=most_rows, fill_value=0)[0].astype(jnp.int32)
        count = jnp.sum(chosen.astype(jnp.int32))
        valid = jnp.arange(most_rows, dtype=jnp.int32) < count
        token = index // 2
        rows = moe_in[token]
        w_gate = lax.dynamic_index_in_dim(gate_proj, expert, 0, keepdims=False)
        w_up = lax.dynamic_index_in_dim(up_proj, expert, 0, keepdims=False)
        w_down = lax.dynamic_index_in_dim(down_proj, expert, 0, keepdims=False)
        gate = jnp.dot(rows, w_gate, preferred_element_type=jnp.float32)
        upper = jnp.dot(rows, w_up, preferred_element_type=jnp.float32)
        hidden = (jax.nn.silu(gate) * upper).astype(jnp.bfloat16)
        result = jnp.dot(hidden, w_down, preferred_element_type=jnp.float32).astype(jnp.bfloat16)
        result = lax.optimization_barrier(result).astype(jnp.float32)
        weight = jnp.where(valid, flat_gates[index], 0.0)
        return (total.at[token].add(result * weight[:, None]), None)
    mixture, unused = lax.scan(expert_step, jnp.zeros((PROMPT_POSITIONS, D), jnp.float32), jnp.arange(EXPERTS, dtype=jnp.int32))
    return (stream32 + mixture).astype(jnp.bfloat16)
```

```python
import jax
import jax.numpy as jnp
from jax import lax
from jax.sharding import Mesh
from jax.sharding import PartitionSpec as P

BF = jnp.bfloat16
F32 = jnp.float32


def swap_core(x):
    return lax.ppermute(x, "core", [(0, 1), (1, 0)])


def shift_z(x, by, wrap=False):
    n = lax.axis_size("z")
    if wrap:
        perm = [(i, (i + by) % n) for i in range(n)]
    else:
        perm = [(i, i + by) for i in range(n) if 0 <= i + by < n]
    return lax.ppermute(x, "z", perm)


def to_expert(x, k):
    n = lax.axis_size("expert")
    return lax.ppermute(x, "expert", [(i, i ^ k) for i in range(n)])


def by_core(core, own, other):
    first = core == 0
    return jnp.where(first, own, other), jnp.where(first, other, own)


def line_gather(x):
    n = lax.axis_size("z")
    z = lax.axis_index("z")
    right, left = [x], [x]
    for _ in range(n - 1):
        right.append(shift_z(right[-1], 1))
        left.append(shift_z(left[-1], -1))
    return [x] + [jnp.where(z >= k, right[k], left[n - k]) for k in range(1, n)]


def absolute(pieces, axis):
    n = len(pieces)
    z = lax.axis_index("z")
    stacked = jnp.stack(pieces)
    return jnp.concatenate(
        [
            lax.dynamic_index_in_dim(stacked, lax.rem(z - s + n, n), 0, keepdims=False)
            for s in range(n)
        ],
        axis=axis,
    )


def attention(queries, keys, values, decay_rate, start_state):
    core, z, n_z = lax.axis_index("core"), lax.axis_index("z"), lax.axis_size("z")
    heads, head_dim = start_state.shape[:2]
    length = queries.shape[0]
    queries = queries.reshape(length, heads, head_dim)
    keys = keys.reshape(length, heads, head_dim)
    values = values.reshape(length, heads, head_dim)
    positions = jnp.arange(length)
    upto = positions[:, None] <= positions[None, :]
    cum = jnp.dot(decay_rate, upto.astype(F32), precision=lax.Precision.HIGHEST)
    total = cum[:, -1]
    scaled_keys = keys.astype(F32) * jnp.exp(cum - total[:, None]).T[:, :, None]
    local = jnp.einsum(
        "shd,she->hde", scaled_keys, values.astype(F32), precision=lax.Precision.HIGHEST
    )
    other_total, other_local = swap_core(total), swap_core(local.astype(BF)).astype(F32)
    total0, total1 = by_core(core, total, other_total)
    half = heads // 2

    def mine(x):
        return lax.dynamic_slice_in_dim(x, core * half, half, 0)

    own_half, other_half = mine(local), mine(other_local)
    local0, local1 = by_core(core, own_half, other_half)
    chip_total = total0 + total1
    chip_state = (jnp.exp(-mine(total1))[:, None, None] * local0 + local1).astype(BF)
    earlier_states = [shift_z(chip_state, k) for k in range(1, n_z)]
    earlier_totals = [shift_z(chip_total, k) for k in range(1, n_z)]

    causal = upto.T[None, :, :]
    diff = cum[:, None, :] - cum[:, :, None]
    decay = jnp.where(causal, jnp.exp(jnp.where(causal, diff, 0.0)), 0.0)
    scores = jnp.einsum("thd,shd->hts", queries, keys, preferred_element_type=F32)
    weights = (scores * decay).astype(BF)
    intra = jnp.einsum("hts,shd->thd", weights, values, preferred_element_type=F32)

    passed = jnp.zeros_like(total)
    incoming = jnp.zeros((half, head_dim, head_dim), F32)
    for state, decayed in zip(earlier_states, earlier_totals):
        incoming = incoming + jnp.exp(-mine(passed))[:, None, None] * state.astype(F32)
        passed = passed + decayed
    incoming = incoming + jnp.exp(-mine(passed))[:, None, None] * mine(start_state)
    incoming = incoming.astype(BF)
    in0, in1 = by_core(core, incoming, swap_core(incoming))
    incoming = jnp.concatenate([in0, in1], axis=0).astype(F32)
    incoming = jnp.where(
        core == 0, incoming, jnp.exp(-total0)[:, None, None] * incoming + other_local
    )
    inter = jnp.einsum(
        "thd,hde->the", queries.astype(F32), incoming, precision=lax.Precision.HIGHEST
    )
    attended = intra + inter * jnp.exp(-cum).T[:, :, None]
    scale = lax.rsqrt(jnp.mean(attended * attended, axis=-1, keepdims=True) + 1e-06)
    return (attended * scale).astype(BF).reshape(length, heads * head_dim)


def shards(
    residual,
    attn_queries,
    attn_keys,
    attn_values,
    decay_rate,
    start_state,
    out_proj,
    moe_gain,
    gate_proj,
    up_proj,
    down_proj,
    expert_ids,
    expert_gates,
):
    n_z, n_exp = lax.axis_size("z"), lax.axis_size("expert")
    z, core, expert = lax.axis_index("z"), lax.axis_index("core"), lax.axis_index("expert")
    rows, width = residual.shape
    part = width // n_z
    capacity = 3 * rows // n_exp

    w_out = jnp.concatenate(by_core(core, out_proj, swap_core(out_proj)), axis=1)
    gate_t, up_t = gate_proj[0].T, up_proj[0].T
    w_in = jnp.concatenate(
        by_core(core, gate_t, swap_core(gate_t)) + by_core(core, up_t, swap_core(up_t)), axis=0
    )
    down = down_proj[0]
    w_down = jnp.concatenate(by_core(core, down, swap_core(down)), axis=1)

    named = jnp.concatenate([expert_ids.astype(F32), expert_gates], axis=1)
    named = absolute([named[None]] + [shift_z(named[None], k, True) for k in range(1, n_z)], 0)
    ids, gates = named[:, :, :2].astype(jnp.int32), named[:, :, 2:]
    blocks = residual.reshape(rows, n_z, part)

    def columns_of(k):
        return lax.dynamic_index_in_dim(blocks, lax.rem(z + k, n_z), 1, keepdims=False)

    kept = [columns_of(0)] + [shift_z(columns_of(k), k, True) for k in range(1, n_z)]

    partner = expert ^ jnp.arange(n_exp)
    names = ids[:, :, :, None] == partner
    member = jnp.any(names, axis=2)
    before = jnp.arange(rows)[None, :] < jnp.arange(rows)[:, None]
    slot = jnp.einsum(
        "tu,suk->stk", before.astype(BF), member.astype(BF), preferred_element_type=F32
    ).astype(jnp.int32)
    places = jnp.arange(capacity)
    placed = member[:, :, :, None] & (slot[:, :, :, None] == places)
    chosen = names[:, :, :, :, None] & (slot[:, :, None, :, None] == places)
    chosen = chosen.astype(BF).reshape(n_z, rows, 2, n_exp * capacity)

    head_out = attention(attn_queries, attn_keys, attn_values, decay_rate, start_state)
    gathered = jnp.stack(line_gather(head_out)).reshape(n_z, n_exp, rows, -1)

    def projected_for(k):
        block = lax.dynamic_index_in_dim(gathered, expert ^ k, 1, keepdims=False)
        return jnp.einsum("std,df->stf", block, w_out, preferred_element_type=F32).astype(BF)

    summed = jnp.zeros((n_z, rows, part), F32)
    for k in reversed(range(n_exp)):
        piece = projected_for(k)
        summed = summed + (to_expert(piece, k) if k else piece).astype(F32)
    stream = (jnp.stack(kept).astype(F32) + summed).astype(BF)
    stream = absolute(list(stream[:, None]), 0)

    full = absolute(line_gather(stream), 2).astype(F32)
    moe_in = (
        full * lax.rsqrt(jnp.mean(full * full, axis=-1, keepdims=True) + 1e-06) * moe_gain
    ).astype(BF)

    routed = []
    for k in reversed(range(n_exp)):
        block = jnp.einsum(
            "stc,std->scd",
            placed[:, :, k].astype(BF),
            moe_in,
            preferred_element_type=F32,
        ).astype(BF)
        routed.append(to_expert(block, k) if k else block)
    routed = jnp.stack(routed[::-1]).reshape(-1, width)

    pre = jnp.einsum("rd,fd->rf", routed, w_in, preferred_element_type=F32)
    units = pre.shape[1] // 2
    hidden = (jax.nn.silu(pre[:, :units]) * pre[:, units:]).astype(BF)
    w_down = w_down.reshape(n_z, units, part)
    expert_out = jnp.zeros((hidden.shape[0], part), F32)
    for k, piece in enumerate(line_gather(hidden)):
        w = lax.dynamic_index_in_dim(w_down, lax.rem(z - k + n_z, n_z), 0, keepdims=False)
        expert_out = expert_out + jnp.dot(piece, w, preferred_element_type=F32)
    expert_out = expert_out.astype(BF).reshape(n_exp, n_z, capacity, part)

    returned = [to_expert(expert_out[k], k) if k else expert_out[k] for k in range(n_exp)]
    returned = jnp.stack(returned, axis=1).reshape(n_z, n_exp * capacity, part)
    out = stream.astype(F32)
    for j in range(2):
        picked = jnp.einsum("str,srd->std", chosen[:, :, j], returned, preferred_element_type=F32)
        out = out + picked * gates[:, :, j, None]
    out = out.astype(BF)

    def rows_of(k):
        return lax.dynamic_index_in_dim(out, lax.rem(z + k, n_z), 0, keepdims=False)

    return absolute([rows_of(0)] + [shift_z(rows_of(k), k, True) for k in range(1, n_z)], 1)


def solution(mesh):
    n_ctx, n_exp = mesh.shape["context"], mesh.shape["expert"]
    fine = Mesh(mesh.devices.reshape(n_ctx // 2, 2, n_exp), ("z", "core", "expert"))
    ctx = ("z", "core")
    owner = ("z", "core", "expert")
    placed = (
        P(owner, None),
        P(ctx, "expert"),
        P(ctx, "expert"),
        P(ctx, "expert"),
        P("expert", ctx),
        P("expert", None, None),
        P("expert", ctx),
        P(),
        P("expert", None, ctx),
        P("expert", None, ctx),
        P("expert", None, ctx),
        P(owner, None),
        P(owner, None),
    )
    return jax.shard_map(
        shards, mesh=fine, in_specs=placed, out_specs=P(owner, None), check_vma=False
    )
```

```python
import jax
import jax.numpy as jnp
from jax import lax
from jax.experimental import pallas as pl
from jax.experimental.pallas import tpu as pltpu
from jax.sharding import Mesh
from jax.sharding import PartitionSpec as P

BF = jnp.bfloat16
F32 = jnp.float32
CHUNKS = 2


def after(x, *first):
    return lax.optimization_barrier((x, first))[0]


def swap_core(x):
    return lax.ppermute(x, "core", [(0, 1), (1, 0)])


def shift_z(x, by, wrap=False):
    n = lax.axis_size("z")
    if wrap:
        perm = [(i, (i + by) % n) for i in range(n)]
    else:
        perm = [(i, i + by) for i in range(n) if 0 <= i + by < n]
    return lax.ppermute(x, "z", perm)


def to_expert(x, k):
    n = lax.axis_size("expert")
    return lax.ppermute(x, "expert", [(i, i ^ k) for i in range(n)])


def by_core(core, own, other):
    first = core == 0
    return jnp.where(first, own, other), jnp.where(first, other, own)


def line_gather(x, relay=lambda x: x):
    n = lax.axis_size("z")
    right, left = [x], [x]
    for step in range(n - 1):
        right.append(shift_z(right[-1] if step != 1 else relay(right[-1]), 1))
        left.append(shift_z(left[-1], -1))
    return right[:0:-1] + left


def copy_shard(z, n, s, pieces, rows, target, sem):
    for i in range(s, s + n):

        @pl.when(n - 1 + s - z == i)
        def _(i=i):
            source = pieces[i] if rows is None else pieces[i].at[rows]
            pltpu.make_async_copy(source, target, sem).start()


ANY = pl.BlockSpec(memory_space=pl.ANY)
VMEM = pl.BlockSpec(memory_space=pltpu.VMEM)
SMEM = pl.BlockSpec(memory_space=pltpu.SMEM)


def params(megabytes):
    return pltpu.CompilerParams(vmem_limit_bytes=megabytes << 20)


def where_am_i():
    return jnp.stack([lax.axis_index(a) for a in ("z", "core", "expert")]).astype(jnp.int32)


def project_kernel(block, n, n_exp, rows, me, *refs):
    pieces, (own, other, *outs) = refs[: 2 * n - 1], refs[2 * n - 1 :]
    outs, (x, w, x_sem, w_sem) = outs[:n_exp], outs[n_exp:]
    z, core, expert = me[0], me[1], me[2]
    cols = own.shape[1]
    copies = []
    for i, source in enumerate((own, other)):
        at = pl.multiple_of((core ^ i) * cols, 128)
        copies.append(pltpu.make_async_copy(source, w.at[:, pl.ds(at, cols)], w_sem.at[i]))
        copies[-1].start()
    for k in range(n_exp):
        taken = pl.ds(pl.multiple_of((expert ^ k) * rows, 16), rows)
        for i, s in enumerate(block):
            to = x.at[pl.ds((k * len(block) + i) * rows, rows)]
            copy_shard(z, n, s, pieces, taken, to, x_sem.at[k * len(block) + i])
    for c in copies:
        c.wait()
    for i in range(n_exp * len(block)):
        to = x.at[pl.ds(i * rows, rows)]
        pltpu.make_async_copy(pieces[0].at[pl.ds(0, rows)], to, x_sem.at[i]).wait()
    size = rows * len(block)
    for k in range(n_exp):
        outs[k][...] = jnp.dot(
            x[pl.ds(k * size, size), :], w[...], preferred_element_type=F32
        ).astype(BF)


def project_call(block, n, n_exp, rows, pieces, own, other):
    size = rows * len(block)
    depth, cols = own.shape
    flops = 4 * n_exp * size * depth * cols
    return pl.pallas_call(
        lambda *refs: project_kernel(block, n, n_exp, rows, *refs),
        name="project",
        out_shape=[jax.ShapeDtypeStruct((size, 2 * cols), BF)] * n_exp,
        in_specs=[SMEM] + [ANY] * (2 * n + 1),
        out_specs=[VMEM] * n_exp,
        scratch_shapes=[
            pltpu.VMEM((n_exp * size, depth), BF),
            pltpu.VMEM((depth, 2 * cols), BF),
            pltpu.SemaphoreType.DMA((n_exp * len(block),)),
            pltpu.SemaphoreType.DMA((2,)),
        ],
        compiler_params=params(32),
        cost_estimate=pl.CostEstimate(flops=flops, transcendentals=0, bytes_accessed=12 << 20),
    )(where_am_i(), *pieces, own, other)


def route_kernel(n, n_exp, me, *refs):
    pieces, (gain, picks, *outs) = refs[: 2 * n - 1], refs[2 * n - 1 :]
    outs, (x, sem) = outs[:n_exp], outs[n_exp:]
    part = pieces[0].shape[1]
    for s in range(n):
        copy_shard(me[0], n, s, pieces, None, x.at[:, pl.ds(s * part, part)], sem.at[s])
    for s in range(n):
        pltpu.make_async_copy(pieces[0], x.at[:, pl.ds(s * part, part)], sem.at[s]).wait()
    full = x[...].astype(F32)
    scale = lax.rsqrt(jnp.mean(full * full, axis=-1, keepdims=True) + 1e-06)
    moe_in = (full * scale * gain[...]).astype(BF)
    for k in range(n_exp):
        outs[k][...] = jnp.dot(picks[k], moe_in, preferred_element_type=F32).astype(BF)


def route_call(n, pieces, gain, picks):
    n_exp, taken, size = picks.shape
    width = n * pieces[0].shape[1]
    return pl.pallas_call(
        lambda *refs: route_kernel(n, n_exp, *refs),
        name="route",
        out_shape=[jax.ShapeDtypeStruct((taken, width), BF)] * n_exp,
        in_specs=[SMEM] + [ANY] * (2 * n - 1) + [VMEM] * 2,
        out_specs=[VMEM] * n_exp,
        scratch_shapes=[pltpu.VMEM((size, width), BF), pltpu.SemaphoreType.DMA((n,))],
        compiler_params=params(32),
        cost_estimate=pl.CostEstimate(
            flops=2 * n_exp * taken * size * width, transcendentals=0, bytes_accessed=12 << 20
        ),
    )(where_am_i(), *pieces, gain, picks)


def gate_up_kernel(count, tiles, me, *refs):
    pieces, weights, (out, x, w, acc, x_sem, w_sem) = (
        refs[:count],
        refs[count : count + 4],
        refs[count + 4 :],
    )
    core = me[1]
    units, deep = weights[0].shape
    tile = deep // tiles
    each = pieces[0].shape[0]

    def copies(t):
        made = []
        for i, source in enumerate(weights):
            at = pl.multiple_of((i // 2) * 2 * units + (core ^ (i % 2)) * units, 16)
            made.append(
                pltpu.make_async_copy(
                    source.at[:, pl.ds(t * tile, tile)],
                    w.at[t % 2, pl.ds(at, units)],
                    w_sem.at[t % 2, i],
                )
            )
        return made

    moves = [
        pltpu.make_async_copy(p, x.at[pl.ds(i * each, each)], x_sem.at[i])
        for i, p in enumerate(pieces)
    ]
    for c in copies(0) + moves + copies(1):
        c.start()
    for c in moves:
        c.wait()
    for t in range(tiles):
        for c in copies(t):
            c.wait()
        product = lax.dot_general(
            x[:, pl.ds(t * tile, tile)],
            w[t % 2],
            (((1,), (1,)), ((), ())),
            preferred_element_type=F32,
        )
        acc[...] = product if t == 0 else acc[...] + product
        if t + 2 < tiles:
            for c in copies(t + 2):
                c.start()
    gate, up = acc[:, : 2 * units], acc[:, 2 * units :]
    out[...] = (gate / (1.0 + jnp.exp(-gate)) * up).astype(BF)


def gate_up_call(pieces, weights):
    units, deep = weights[0].shape
    if pieces[0].shape[0] % 16:
        pieces = [jnp.concatenate(pieces, axis=0)]
    size = len(pieces) * pieces[0].shape[0]
    tiles = 4
    return pl.pallas_call(
        lambda *refs: gate_up_kernel(len(pieces), tiles, *refs),
        name="gate_up",
        out_shape=jax.ShapeDtypeStruct((size, 2 * units), BF),
        in_specs=[SMEM] + [ANY] * (len(pieces) + 4),
        out_specs=VMEM,
        scratch_shapes=[
            pltpu.VMEM((size, deep), BF),
            pltpu.VMEM((2, 4 * units, deep // tiles), BF),
            pltpu.VMEM((size, 4 * units), F32),
            pltpu.SemaphoreType.DMA((len(pieces),)),
            pltpu.SemaphoreType.DMA((2, 4)),
        ],
        compiler_params=params(48),
        cost_estimate=pl.CostEstimate(
            flops=8 * size * deep * units,
            transcendentals=2 * size * units,
            bytes_accessed=8 * units * deep + 2 * size * deep,
        ),
    )(where_am_i(), *pieces, *weights)


def down_kernel(n, count, me, *refs):
    pieces, (own, other, *outs) = refs[: 2 * n - 1], refs[2 * n - 1 :]
    outs, (x, w, acc, x_sem, w_sem) = outs[:count], outs[count:]
    z, core = me[0], me[1]
    cols = own.shape[1]
    deep = own.shape[0] // n

    def copies(s):
        return [
            pltpu.make_async_copy(
                source.at[pl.ds(s * deep, deep)],
                w.at[s, :, pl.ds(pl.multiple_of((core ^ i) * cols, 128), cols)],
                w_sem.at[s, i],
            )
            for i, source in enumerate((own, other))
        ]

    for s in range(n):
        copy_shard(z, n, s, pieces, None, x.at[s], x_sem.at[s])
        for c in copies(s):
            c.start()
    for s in range(n):
        pltpu.make_async_copy(pieces[0], x.at[s], x_sem.at[s]).wait()
        for c in copies(s):
            c.wait()
        product = jnp.dot(x[s], w[s], preferred_element_type=F32)
        acc[...] = product if s == 0 else acc[...] + product
    each = acc.shape[0] // count
    for i in range(count):
        outs[i][...] = acc[pl.ds(i * each, each), :].astype(BF)


def down_call(n, n_exp, pieces, own, other):
    size, deep = pieces[0].shape
    cols = own.shape[1]
    count = n_exp if size // n_exp % 16 == 0 else 1
    outs = pl.pallas_call(
        lambda *refs: down_kernel(n, count, *refs),
        name="down",
        out_shape=[jax.ShapeDtypeStruct((size // count, 2 * cols), BF)] * count,
        in_specs=[SMEM] + [ANY] * (2 * n + 1),
        out_specs=[VMEM] * count,
        scratch_shapes=[
            pltpu.VMEM((n, size, deep), BF),
            pltpu.VMEM((n, deep, 2 * cols), BF),
            pltpu.VMEM((size, 2 * cols), F32),
            pltpu.SemaphoreType.DMA((n,)),
            pltpu.SemaphoreType.DMA((n, 2)),
        ],
        compiler_params=params(40),
        cost_estimate=pl.CostEstimate(
            flops=4 * n * size * deep * cols, transcendentals=0, bytes_accessed=20 << 20
        ),
    )(where_am_i(), *pieces, own, other)
    return outs if count == n_exp else list(outs[0].reshape(n_exp, -1, 2 * cols))


def absolute(pieces, axis):
    n = len(pieces)
    z = lax.axis_index("z")
    stacked = jnp.stack(pieces)
    return jnp.concatenate(
        [
            lax.dynamic_index_in_dim(stacked, lax.rem(z - s + n, n), 0, keepdims=False)
            for s in range(n)
        ],
        axis=axis,
    )


def attention(queries, keys, values, decay_rate, start_state, first):
    core, z, n_z = lax.axis_index("core"), lax.axis_index("z"), lax.axis_size("z")
    heads, head_dim = start_state.shape[:2]
    length = queries.shape[0]
    queries = queries.reshape(length, heads, head_dim)
    keys = keys.reshape(length, heads, head_dim)
    values = values.reshape(length, heads, head_dim)
    positions = jnp.arange(length)
    upto = positions[:, None] <= positions[None, :]
    cum = jnp.dot(decay_rate, upto.astype(F32), precision=lax.Precision.HIGHEST)
    total = cum[:, -1]
    scaled_keys = keys.astype(F32) * jnp.exp(cum - total[:, None]).T[:, :, None]
    local = jnp.einsum(
        "shd,she->hde", scaled_keys, values.astype(F32), precision=lax.Precision.HIGHEST
    )
    other_total, other_local = swap_core(total), swap_core(local.astype(BF)).astype(F32)
    total0, total1 = by_core(core, total, other_total)
    half = heads // 2

    def mine(x):
        return lax.dynamic_slice_in_dim(x, core * half, half, 0)

    own_half, other_half = mine(local), mine(other_local)
    local0, local1 = by_core(core, own_half, other_half)
    chip_total = total0 + total1
    chip_state = (jnp.exp(-mine(total1))[:, None, None] * local0 + local1).astype(BF)
    chip_state = after(chip_state, first)
    earlier_states = [shift_z(chip_state, k) for k in range(1, n_z)]
    earlier_totals = [shift_z(chip_total, k) for k in range(1, n_z)]

    causal = upto.T[None, :, :]
    diff = cum[:, None, :] - cum[:, :, None]
    decay = jnp.where(causal, jnp.exp(jnp.where(causal, diff, 0.0)), 0.0)
    scores = jnp.einsum("thd,shd->hts", queries, keys, preferred_element_type=F32)
    weights = (scores * decay).astype(BF)
    intra = jnp.einsum("hts,shd->thd", weights, values, preferred_element_type=F32)

    passed = jnp.zeros_like(total)
    incoming = jnp.zeros((half, head_dim, head_dim), F32)
    for state, decayed in zip(earlier_states, earlier_totals):
        incoming = incoming + jnp.exp(-mine(passed))[:, None, None] * state.astype(F32)
        passed = passed + decayed
    incoming = incoming + jnp.exp(-mine(passed))[:, None, None] * mine(start_state)
    incoming = incoming.astype(BF)
    in0, in1 = by_core(core, incoming, swap_core(incoming))
    incoming = jnp.concatenate([in0, in1], axis=0).astype(F32)
    incoming = jnp.where(
        core == 0, incoming, jnp.exp(-total0)[:, None, None] * incoming + other_local
    )
    inter = jnp.einsum(
        "thd,hde->the", queries.astype(F32), incoming, precision=lax.Precision.HIGHEST
    )
    attended = intra + inter * jnp.exp(-cum).T[:, :, None]
    scale = lax.rsqrt(jnp.mean(attended * attended, axis=-1, keepdims=True) + 1e-06)
    return (attended * scale).astype(BF).reshape(length, heads * head_dim)


def shards(
    residual,
    attn_queries,
    attn_keys,
    attn_values,
    decay_rate,
    start_state,
    out_proj,
    moe_gain,
    gate_proj,
    up_proj,
    down_proj,
    expert_ids,
    expert_gates,
):
    n_z, n_exp = lax.axis_size("z"), lax.axis_size("expert")
    z, core, expert = lax.axis_index("z"), lax.axis_index("core"), lax.axis_index("expert")
    rows, width = residual.shape
    part = width // n_z
    capacity = 3 * rows // n_exp

    w_out, w_gate, w_up, w_down = [
        (w, swap_core(w)) for w in (out_proj, gate_proj[0].T, up_proj[0].T, down_proj[0])
    ]

    named = jnp.concatenate([expert_ids.astype(F32), expert_gates], axis=1)
    named = absolute([named[None]] + [shift_z(named[None], k, True) for k in range(1, n_z)], 0)
    ids, gates = named[:, :, :2].astype(jnp.int32), named[:, :, 2:]
    blocks = residual.reshape(rows, n_z, part)

    def columns_of(k):
        return lax.dynamic_index_in_dim(blocks, lax.rem(z + k, n_z), 1, keepdims=False)

    kept = [columns_of(0)] + [shift_z(columns_of(k), k, True) for k in range(1, n_z)]
    kept = absolute(kept, 0).reshape(n_z, rows, part)

    partner = expert ^ jnp.arange(n_exp)
    names = ids[:, :, :, None] == partner
    member = jnp.any(names, axis=2)
    before = jnp.arange(rows)[None, :] < jnp.arange(rows)[:, None]
    slot = jnp.einsum(
        "tu,suk->stk", before.astype(BF), member.astype(BF), preferred_element_type=F32
    ).astype(jnp.int32)
    places = jnp.arange(capacity)
    placed = member[:, :, :, None] & (slot[:, :, :, None] == places)
    chosen = names[:, :, :, :, None] & (slot[:, :, None, :, None] == places)
    chosen = chosen.astype(BF).reshape(n_z, rows, 2, n_exp * capacity)

    head_out = attention(
        attn_queries, attn_keys, attn_values, decay_rate, start_state, (named,)
    )
    head_out = after(head_out, kept)
    acts = line_gather(head_out)
    gain = moe_gain.reshape(1, width)

    def of_block(x, block):
        return jnp.stack([x[s] for s in block])

    def project(block, first):
        pieces = project_call(block, n_z, n_exp, rows, acts, *w_out)
        arrived = [pieces[0]] + [
            to_expert(after(pieces[k], first), k) for k in range(1, n_exp)
        ]
        total = jnp.concatenate([kept[s] for s in block], axis=0).astype(F32)
        for x in arrived:
            total = total + x.astype(F32)
        return total.astype(BF), arrived

    def route(block, pieces, first):
        placed_here = of_block(placed, block)
        eye = jnp.eye(len(block), dtype=bool)[None, :, None, :, None]
        picks = placed_here.transpose(2, 0, 3, 1)[:, :, :, None, :] & eye
        picks = picks.astype(BF).reshape(n_exp, len(block) * capacity, len(block) * rows)
        sent = route_call(n_z, pieces, gain, picks)
        return sent, [sent[0]] + [
            to_expert(after(sent[k], first), k) for k in range(1, n_exp)
        ]

    def combine(block, stream, hidden):
        expert_out = down_call(n_z, n_exp, hidden, *w_down)
        returned = [to_expert(expert_out[k], k) if k else expert_out[k] for k in range(n_exp)]
        returned = [x.reshape(len(block), capacity, part) for x in returned]
        returned = jnp.concatenate(returned, axis=1)
        out = stream.reshape(len(block), rows, part).astype(F32)
        for j in range(2):
            picked = jnp.einsum(
                "str,srd->std",
                of_block(chosen, block)[:, :, j],
                returned,
                preferred_element_type=F32,
            )
            out = out + picked * of_block(gates, block)[:, :, j, None]
        return out.astype(BF)

    middle_first = sorted(range(n_z), key=lambda s: abs(2 * s - n_z + 1))
    size = n_z // CHUNKS
    blocks = [middle_first[start : start + size] for start in range(0, n_z, size)]
    streams, waiting = [], []
    summed = sent = full = routed = hidden = ()
    for block in blocks:
        stream, summed = project(block, summed)
        streams.append(stream)
        full = line_gather(after(stream, full, sent))
        sent, routed = route(block, full, routed)
        stepped = hidden[n_z - 2 : n_z + 1]
        hidden = line_gather(
            after(gate_up_call([after(x, stepped) for x in routed], w_gate + w_up), hidden)
        )
        waiting.append(hidden)
    out = [None] * n_z
    for i, block in enumerate(blocks):
        later = waiting[i + 1][n_z - 2 : n_z + 1] if i + 1 < len(blocks) else ()
        pieces = [after(x, later) for x in waiting[i]]
        for s, piece in zip(block, combine(block, streams[i], pieces)):
            out[s] = piece
    out = jnp.stack(out)

    def rows_of(k):
        return lax.dynamic_index_in_dim(out, lax.rem(z + k, n_z), 0, keepdims=False)

    return absolute([rows_of(0)] + [shift_z(rows_of(k), k, True) for k in range(1, n_z)], 1)


def solution(mesh):
    n_ctx, n_exp = mesh.shape["context"], mesh.shape["expert"]
    fine = Mesh(mesh.devices.reshape(n_ctx // 2, 2, n_exp), ("z", "core", "expert"))
    ctx = ("z", "core")
    owner = ("z", "core", "expert")
    placed = (
        P(owner, None),
        P(ctx, "expert"),
        P(ctx, "expert"),
        P(ctx, "expert"),
        P("expert", ctx),
        P("expert", None, None),
        P("expert", ctx),
        P(),
        P("expert", None, ctx),
        P("expert", None, ctx),
        P("expert", None, ctx),
        P(owner, None),
        P(owner, None),
    )
    return jax.shard_map(
        shards, mesh=fine, in_specs=placed, out_specs=P(owner, None), check_vma=False
    )
```

```python
import jax
import jax.numpy as jnp
from jax import lax
from jax.experimental import pallas as pl
from jax.experimental.pallas import tpu as pltpu
from jax.sharding import Mesh
from jax.sharding import PartitionSpec as P

BF = jnp.bfloat16
F32 = jnp.float32
GROUPS = (2, 1)


def after(x, *first):
    return lax.optimization_barrier((x, first))[0]


def swap_core(x):
    return lax.ppermute(x, "core", [(0, 1), (1, 0)])


def shift_z(x, by, wrap=False):
    n = lax.axis_size("z")
    if wrap:
        perm = [(i, (i + by) % n) for i in range(n)]
    else:
        perm = [(i, i + by) for i in range(n) if 0 <= i + by < n]
    return lax.ppermute(x, "z", perm)


def to_expert(x, k):
    n = lax.axis_size("expert")
    return lax.ppermute(x, "expert", [(i, i ^ k) for i in range(n)])


def by_core(core, own, other):
    first = core == 0
    return jnp.where(first, own, other), jnp.where(first, other, own)


def line_gather(x):
    n = lax.axis_size("z")
    right, left = [x], [x]
    for step in range(n - 1):
        onward = [(i, i + 1) for i in range(step, n - 1)]
        rightward, leftward = lax.optimization_barrier((right[-1], left[-1]))
        right.append(lax.ppermute(rightward, "z", onward))
        left.append(lax.ppermute(leftward, "z", [(n - 1 - i, n - 1 - j) for i, j in onward]))
    return right[:0:-1] + left


def copy_shard(z, n, s, pieces, rows, target, sem, skipped=0):
    for i in range(s, s + n):

        @pl.when(n - 1 + s - z == i)
        def _(piece=pieces[i - skipped]):
            source = piece if rows is None else piece.at[rows]
            pltpu.make_async_copy(source, target, sem).start()


ANY = pl.BlockSpec(memory_space=pltpu.HBM)
VMEM = pl.BlockSpec(memory_space=pltpu.VMEM)
SMEM = pl.BlockSpec(memory_space=pltpu.SMEM)


def params(megabytes):
    return pltpu.CompilerParams(vmem_limit_bytes=megabytes << 20)


def where_am_i():
    return jnp.stack([lax.axis_index(a) for a in ("z", "core", "expert")]).astype(jnp.int32)


def project_kernel(block, n, n_exp, rows, me, *refs):
    count = max(block) + n - min(block)
    pieces, (weights, *outs) = refs[:count], refs[count:]
    outs, (x, w, x_sem, w_sem) = outs[:n_exp], outs[n_exp:]
    z, expert = me[0], me[2]
    cols = weights.shape[2]
    copies = []
    for i in range(2):
        to = w.at[:, pl.ds(i * cols, cols)]
        copies.append(pltpu.make_async_copy(weights.at[i], to, w_sem.at[i]))
        copies[-1].start()
    for k in range(n_exp):
        taken = pl.ds(pl.multiple_of((expert ^ k) * rows, 16), rows)
        for i, s in enumerate(block):
            to = x.at[pl.ds((k * len(block) + i) * rows, rows)]
            copy_shard(z, n, s, pieces, taken, to, x_sem.at[k * len(block) + i], min(block))
    for c in copies:
        c.wait()
    for i in range(n_exp * len(block)):
        to = x.at[pl.ds(i * rows, rows)]
        pltpu.make_async_copy(pieces[0].at[pl.ds(0, rows)], to, x_sem.at[i]).wait()
    size = rows * len(block)
    for k in range(n_exp):
        outs[k][...] = jnp.dot(
            x[pl.ds(k * size, size), :], w[...], preferred_element_type=F32
        ).astype(BF)


def project_call(block, n, n_exp, rows, pieces, weights):
    size = rows * len(block)
    depth, cols = weights.shape[1:]
    pieces = pieces[min(block) : max(block) + n]
    flops = 4 * n_exp * size * depth * cols
    return pl.pallas_call(
        lambda *refs: project_kernel(block, n, n_exp, rows, *refs),
        name="project",
        out_shape=[jax.ShapeDtypeStruct((size, 2 * cols), BF)] * n_exp,
        in_specs=[SMEM] + [ANY] * (len(pieces) + 1),
        out_specs=[VMEM] * n_exp,
        scratch_shapes=[
            pltpu.VMEM((n_exp * size, depth), BF),
            pltpu.VMEM((depth, 2 * cols), BF),
            pltpu.SemaphoreType.DMA((n_exp * len(block),)),
            pltpu.SemaphoreType.DMA((2,)),
        ],
        compiler_params=params(32),
        cost_estimate=pl.CostEstimate(flops=flops, transcendentals=0, bytes_accessed=12 << 20),
    )(where_am_i(), *pieces, weights)


def route_kernel(n, groups, me, *refs):
    pieces, (gain, *refs) = refs[: 2 * n - 1], refs[2 * n - 1 :]
    picks, outs, (x, sem) = refs[:groups], refs[groups:-2], refs[-2:]
    part = pieces[0].shape[1]
    for s in range(n):
        copy_shard(me[0], n, s, pieces, None, x.at[:, pl.ds(s * part, part)], sem.at[s])
    for s in range(n):
        pltpu.make_async_copy(pieces[0], x.at[:, pl.ds(s * part, part)], sem.at[s]).wait()
    full = x[...].astype(F32)
    scale = lax.rsqrt(jnp.mean(full * full, axis=-1, keepdims=True) + 1e-06)
    moe_in = (full * scale * gain[...]).astype(BF)
    n_exp = len(outs) // groups
    for i in range(groups):
        for k in range(n_exp):
            outs[i * n_exp + k][...] = jnp.dot(
                picks[i][k], moe_in, preferred_element_type=F32
            ).astype(BF)


def route_call(n, pieces, gain, picks):
    n_exp, _, size = picks[0].shape
    width = n * pieces[0].shape[1]
    sizes = [p.shape[1] for p in picks for _ in range(n_exp)]
    outs = pl.pallas_call(
        lambda *refs: route_kernel(n, len(picks), *refs),
        name="route",
        out_shape=[jax.ShapeDtypeStruct((taken, width), BF) for taken in sizes],
        in_specs=[SMEM] + [ANY] * (2 * n - 1) + [VMEM] * (1 + len(picks)),
        out_specs=[VMEM] * len(sizes),
        scratch_shapes=[pltpu.VMEM((size, width), BF), pltpu.SemaphoreType.DMA((n,))],
        compiler_params=params(32),
        cost_estimate=pl.CostEstimate(
            flops=2 * sum(sizes) * size * width, transcendentals=0, bytes_accessed=12 << 20
        ),
    )(where_am_i(), *pieces, gain, *picks)
    return [outs[i : i + n_exp] for i in range(0, len(outs), n_exp)]


def gate_up_kernel(count, tiles, *refs):
    pieces, weights, (out, x, w, acc, x_sem, w_sem) = (
        refs[:count],
        refs[count : count + 2],
        refs[count + 2 :],
    )
    units, deep = weights[0].shape[1:]
    tile = deep // tiles
    each = pieces[0].shape[0]

    def copies(t):
        made = []
        for i in range(4):
            made.append(
                pltpu.make_async_copy(
                    weights[i // 2].at[i % 2, :, pl.ds(t * tile, tile)],
                    w.at[t % 2, pl.ds(i * units, units)],
                    w_sem.at[t % 2, i],
                )
            )
        return made

    moves = [
        pltpu.make_async_copy(p, x.at[pl.ds(i * each, each)], x_sem.at[i])
        for i, p in enumerate(pieces)
    ]
    for c in copies(0) + moves + copies(1):
        c.start()
    for c in moves:
        c.wait()
    for t in range(tiles):
        for c in copies(t):
            c.wait()
        product = lax.dot_general(
            x[:, pl.ds(t * tile, tile)],
            w[t % 2],
            (((1,), (1,)), ((), ())),
            preferred_element_type=F32,
        )
        acc[...] = product if t == 0 else acc[...] + product
        if t + 2 < tiles:
            for c in copies(t + 2):
                c.start()
    gate, up = acc[:, : 2 * units], acc[:, 2 * units :]
    out[...] = (gate / (1.0 + jnp.exp(-gate)) * up).astype(BF)


def gate_up_call(pieces, weights):
    units, deep = weights[0].shape[1:]
    if pieces[0].shape[0] % 16:
        pieces = [jnp.concatenate(pieces, axis=0)]
    size = len(pieces) * pieces[0].shape[0]
    tiles = 4
    return pl.pallas_call(
        lambda *refs: gate_up_kernel(len(pieces), tiles, *refs),
        name="gate_up",
        out_shape=jax.ShapeDtypeStruct((size, 2 * units), BF),
        in_specs=[ANY] * (len(pieces) + 2),
        out_specs=VMEM,
        scratch_shapes=[
            pltpu.VMEM((size, deep), BF),
            pltpu.VMEM((2, 4 * units, deep // tiles), BF),
            pltpu.VMEM((size, 4 * units), F32),
            pltpu.SemaphoreType.DMA((len(pieces),)),
            pltpu.SemaphoreType.DMA((2, 4)),
        ],
        compiler_params=params(48),
        cost_estimate=pl.CostEstimate(
            flops=8 * size * deep * units,
            transcendentals=2 * size * units,
            bytes_accessed=8 * units * deep + 2 * size * deep,
        ),
    )(*pieces, *weights)


def down_kernel(n, count, me, *refs):
    pieces, (weights, *outs) = refs[: 2 * n - 1], refs[2 * n - 1 :]
    outs, (x, w, acc, x_sem, w_sem) = outs[:count], outs[count:]
    cols = weights.shape[2]
    deep = weights.shape[1] // n

    def copies(s):
        return [
            pltpu.make_async_copy(
                weights.at[i, pl.ds(s * deep, deep)],
                w.at[s, :, pl.ds(i * cols, cols)],
                w_sem.at[s, i],
            )
            for i in range(2)
        ]

    for s in range(n):
        copy_shard(me[0], n, s, pieces, None, x.at[s], x_sem.at[s])
        for c in copies(s):
            c.start()
    for s in range(n):
        pltpu.make_async_copy(pieces[0], x.at[s], x_sem.at[s]).wait()
        for c in copies(s):
            c.wait()
        product = jnp.dot(x[s], w[s], preferred_element_type=F32)
        acc[...] = product if s == 0 else acc[...] + product
    each = acc.shape[0] // count
    for i in range(count):
        outs[i][...] = acc[pl.ds(i * each, each), :].astype(BF)


def down_call(n, n_exp, pieces, weights):
    size, deep = pieces[0].shape
    cols = weights.shape[2]
    count = n_exp if size // n_exp % 16 == 0 else 1
    outs = pl.pallas_call(
        lambda *refs: down_kernel(n, count, *refs),
        name="down",
        out_shape=[jax.ShapeDtypeStruct((size // count, 2 * cols), BF)] * count,
        in_specs=[SMEM] + [ANY] * (2 * n),
        out_specs=[VMEM] * count,
        scratch_shapes=[
            pltpu.VMEM((n, size, deep), BF),
            pltpu.VMEM((n, deep, 2 * cols), BF),
            pltpu.VMEM((size, 2 * cols), F32),
            pltpu.SemaphoreType.DMA((n,)),
            pltpu.SemaphoreType.DMA((n, 2)),
        ],
        compiler_params=params(40),
        cost_estimate=pl.CostEstimate(
            flops=4 * n * size * deep * cols, transcendentals=0, bytes_accessed=20 << 20
        ),
    )(where_am_i(), *pieces, weights)
    return outs if count == n_exp else list(outs[0].reshape(n_exp, -1, 2 * cols))


def absolute(pieces, axis):
    n = len(pieces)
    z = lax.axis_index("z")
    stacked = jnp.stack(pieces)
    return jnp.concatenate(
        [
            lax.dynamic_index_in_dim(stacked, lax.rem(z - s + n, n), 0, keepdims=False)
            for s in range(n)
        ],
        axis=axis,
    )


def attention(queries, keys, values, decay_rate, start_state, first):
    core, z, n_z = lax.axis_index("core"), lax.axis_index("z"), lax.axis_size("z")
    heads, head_dim = start_state.shape[:2]
    length = queries.shape[0]
    queries = queries.reshape(length, heads, head_dim)
    keys = keys.reshape(length, heads, head_dim)
    values = values.reshape(length, heads, head_dim)
    positions = jnp.arange(length)
    upto = positions[:, None] <= positions[None, :]
    cum = jnp.dot(decay_rate, upto.astype(F32), precision=lax.Precision.HIGHEST)
    total = cum[:, -1]
    scaled_keys = keys.astype(F32) * jnp.exp(cum - total[:, None]).T[:, :, None]
    local = jnp.einsum(
        "shd,she->hde", scaled_keys, values.astype(F32), precision=lax.Precision.HIGHEST
    )
    other_total, other_local = swap_core(total), swap_core(local.astype(BF)).astype(F32)
    total0, total1 = by_core(core, total, other_total)
    half = heads // 2

    def mine(x):
        return lax.dynamic_slice_in_dim(x, core * half, half, 0)

    own_half, other_half = mine(local), mine(other_local)
    local0, local1 = by_core(core, own_half, other_half)
    chip_total = total0 + total1
    chip_state = (jnp.exp(-mine(total1))[:, None, None] * local0 + local1).astype(BF)
    chip_state = after(chip_state, first)
    earlier_states = [shift_z(chip_state, k) for k in range(1, n_z)]
    earlier_totals = [shift_z(chip_total, k) for k in range(1, n_z)]

    causal = upto.T[None, :, :]
    diff = cum[:, None, :] - cum[:, :, None]
    decay = jnp.where(causal, jnp.exp(jnp.where(causal, diff, 0.0)), 0.0)
    scores = jnp.einsum("thd,shd->hts", queries, keys, preferred_element_type=F32)
    weights = (scores * decay).astype(BF)
    intra = jnp.einsum("hts,shd->thd", weights, values, preferred_element_type=F32)

    earlier_states = after(earlier_states, intra)
    passed = jnp.zeros_like(total)
    incoming = jnp.zeros((half, head_dim, head_dim), F32)
    for state, decayed in zip(earlier_states, earlier_totals):
        incoming = incoming + jnp.exp(-mine(passed))[:, None, None] * state.astype(F32)
        passed = passed + decayed
    incoming = incoming + jnp.exp(-mine(passed))[:, None, None] * mine(start_state)
    incoming = incoming.astype(BF)
    in0, in1 = by_core(core, incoming, swap_core(incoming))
    incoming = jnp.concatenate([in0, in1], axis=0).astype(F32)
    incoming = jnp.where(
        core == 0, incoming, jnp.exp(-total0)[:, None, None] * incoming + other_local
    )
    inter = jnp.einsum(
        "thd,hde->the", queries.astype(F32), incoming, precision=lax.Precision.HIGHEST
    )
    attended = intra + inter * jnp.exp(-cum).T[:, :, None]
    scale = lax.rsqrt(jnp.mean(attended * attended, axis=-1, keepdims=True) + 1e-06)
    return (attended * scale).astype(BF).reshape(length, heads * head_dim)


def shards(
    residual,
    attn_queries,
    attn_keys,
    attn_values,
    decay_rate,
    start_state,
    out_proj,
    moe_gain,
    gate_proj,
    up_proj,
    down_proj,
    expert_ids,
    expert_gates,
):
    n_z, n_exp = lax.axis_size("z"), lax.axis_size("expert")
    z, core, expert = lax.axis_index("z"), lax.axis_index("core"), lax.axis_index("expert")
    rows, width = residual.shape
    part = width // n_z
    capacity = 3 * rows // n_exp

    w_out, w_gate, w_up, w_down = [
        lax.all_gather(w, "core") for w in (out_proj, gate_proj[0].T, up_proj[0].T, down_proj[0])
    ]

    named = jnp.concatenate([expert_ids.astype(F32), expert_gates], axis=1)
    named = absolute([named[None]] + [shift_z(named[None], k, True) for k in range(1, n_z)], 0)
    ids, gates = named[:, :, :2].astype(jnp.int32), named[:, :, 2:]

    def columns_of(k):
        return lax.dynamic_slice_in_dim(residual, lax.rem(z + k, n_z) * part, part, axis=1)

    kept = [columns_of(0)] + [shift_z(columns_of(k), k, True) for k in range(1, n_z)]
    kept = absolute(kept, 0).reshape(n_z, rows, part)

    partner = expert ^ jnp.arange(n_exp)
    names = ids[:, :, :, None] == partner
    member = jnp.any(names, axis=2)
    before = jnp.arange(rows)[None, :] < jnp.arange(rows)[:, None]
    slot = jnp.einsum(
        "tu,suk->stk", before.astype(BF), member.astype(BF), preferred_element_type=F32
    ).astype(jnp.int32)
    places = jnp.arange(capacity)
    placed = member[:, :, :, None] & (slot[:, :, :, None] == places)
    chosen = names[:, :, :, :, None] & (slot[:, :, None, :, None] == places)
    chosen = chosen.astype(BF).reshape(n_z, rows, 2, n_exp * capacity)

    head_out = attention(
        attn_queries, attn_keys, attn_values, decay_rate, start_state, (named, kept)
    )
    acts = line_gather(head_out)
    gain = moe_gain.reshape(1, width)

    def of_block(x, block):
        return jnp.stack([x[s] for s in block])

    def project(block, first):
        pieces = project_call(block, n_z, n_exp, rows, acts, w_out)
        arrived = [pieces[0]] + [
            to_expert(after(pieces[k], first), k) for k in range(1, n_exp)
        ]
        total = jnp.concatenate([kept[s] for s in block], axis=0).astype(F32)
        for x in arrived:
            total = total + x.astype(F32)
        return total.astype(BF), arrived

    def route(block, groups, pieces):
        picks = []
        for group in groups:
            here = jnp.array([[s == t for t in block] for s in group])[None, :, None, :, None]
            one = of_block(placed, group).transpose(2, 0, 3, 1)[:, :, :, None, :] & here
            one = one.astype(BF)
            picks.append(one.reshape(n_exp, len(group) * capacity, len(block) * rows))
        return route_call(n_z, pieces, gain, picks)

    def combine(block, stream, hidden):
        expert_out = down_call(n_z, n_exp, hidden, w_down)
        returned = [to_expert(expert_out[k], k) if k else expert_out[k] for k in range(n_exp)]
        returned = [x.reshape(len(block), capacity, part) for x in returned]
        returned = jnp.concatenate(returned, axis=1)
        out = stream.reshape(len(block), rows, part).astype(F32)
        for j in range(2):
            picked = jnp.einsum(
                "str,srd->std",
                of_block(chosen, block)[:, :, j],
                returned,
                preferred_element_type=F32,
            )
            out = out + picked * of_block(gates, block)[:, :, j, None]
        return out.astype(BF)

    middle_first = sorted(range(n_z), key=lambda s: abs(2 * s - n_z + 1))
    size = n_z // len(GROUPS)
    near = slice(n_z - 2, n_z + 1)
    groups, streams, waiting = [], [], []
    summed = sent = full = routed = hidden = ()
    for i, count in enumerate(GROUPS):
        block = middle_first[i * size : (i + 1) * size]
        stream, summed = project(block, summed)
        full = line_gather(after(stream, full, sent))
        fine = [block[j : j + size // count] for j in range(0, size, size // count)]
        sent = route(block, fine, full)
        for group, rows_for in zip(fine, sent):
            routed = [rows_for[0]] + [
                to_expert(after(rows_for[k], routed), k) for k in range(1, n_exp)
            ]
            started = hidden[near]
            made = gate_up_call([after(x, started) for x in routed], (w_gate, w_up))
            hidden = line_gather(after(made, hidden[1:-1]))
            at = [block.index(s) * rows for s in group]
            groups.append(group)
            streams.append(jnp.stack([stream[r : r + rows] for r in at]))
            waiting.append(hidden)
    out = [None] * n_z
    for i, group in enumerate(groups):
        later = waiting[i + 1][near] if i + 1 < len(groups) else ()
        pieces = [after(x, later) for x in waiting[i]]
        for s, piece in zip(group, combine(group, streams[i], pieces)):
            out[s] = piece
    out = jnp.stack(out)

    def rows_of(k):
        return lax.dynamic_index_in_dim(out, lax.rem(z + k, n_z), 0, keepdims=False)

    return absolute([rows_of(0)] + [shift_z(rows_of(k), k, True) for k in range(1, n_z)], 1)


def solution(mesh):
    n_ctx, n_exp = mesh.shape["context"], mesh.shape["expert"]
    fine = Mesh(mesh.devices.reshape(n_ctx // 2, 2, n_exp), ("z", "core", "expert"))
    ctx = ("z", "core")
    owner = ("z", "core", "expert")
    placed = (
        P(owner, None),
        P(ctx, "expert"),
        P(ctx, "expert"),
        P(ctx, "expert"),
        P("expert", ctx),
        P("expert", None, None),
        P("expert", ctx),
        P(),
        P("expert", None, ctx),
        P("expert", None, ctx),
        P("expert", None, ctx),
        P(owner, None),
        P(owner, None),
    )
    return jax.shard_map(
        shards, mesh=fine, in_specs=placed, out_specs=P(owner, None), check_vma=False
    )
```

```python
import jax
import jax.numpy as jnp
from jax import lax
from jax.experimental import pallas as pl
from jax.experimental.pallas import tpu as pltpu
from jax.sharding import Mesh
from jax.sharding import PartitionSpec as P

BF = jnp.bfloat16
F32 = jnp.float32
GROUPS = (2, 1)


def after(x, *first):
    return lax.optimization_barrier((x, first))[0]


def swap_core(x):
    return lax.ppermute(x, "core", [(0, 1), (1, 0)])


def shift_z(x, by, wrap=False):
    n = lax.axis_size("z")
    if wrap:
        perm = [(i, (i + by) % n) for i in range(n)]
    else:
        perm = [(i, i + by) for i in range(n) if 0 <= i + by < n]
    return lax.ppermute(x, "z", perm)


def to_expert(x, k):
    n = lax.axis_size("expert")
    return lax.ppermute(x, "expert", [(i, i ^ k) for i in range(n)])


def by_core(core, own, other):
    first = core == 0
    return jnp.where(first, own, other), jnp.where(first, other, own)


def line_gather(x, pending=(), work=None):
    n = lax.axis_size("z")
    right, left, made = [x], [x], []
    for step in range(n - 1):
        onward = [(i, i + 1) for i in range(step, n - 1)]
        held = (right[-1], left[-1])
        if made and len(made) == step:
            held, made[-1] = lax.optimization_barrier((held, made[-1]))
        elif step:
            held = lax.optimization_barrier(held)
        now = None
        if step < len(pending):
            held, now = lax.optimization_barrier((held, pending[step]))
        right.append(lax.ppermute(held[0], "z", onward))
        left.append(lax.ppermute(held[1], "z", [(n - 1 - i, n - 1 - j) for i, j in onward]))
        if now is not None:
            made.append(work(now))
    made += [work(x) for x in pending[n - 1 :]]
    return right[:0:-1] + left, made


def copy_shard(z, n, s, pieces, rows, target, sem, skipped=0):
    for i in range(s, s + n):

        @pl.when(n - 1 + s - z == i)
        def _(piece=pieces[i - skipped]):
            source = piece if rows is None else piece.at[rows]
            pltpu.make_async_copy(source, target, sem).start()


ANY = pl.BlockSpec(memory_space=pltpu.HBM)
VMEM = pl.BlockSpec(memory_space=pltpu.VMEM)
SMEM = pl.BlockSpec(memory_space=pltpu.SMEM)


def params(megabytes):
    return pltpu.CompilerParams(vmem_limit_bytes=megabytes << 20)


def where_am_i():
    return jnp.stack([lax.axis_index(a) for a in ("z", "core", "expert")]).astype(jnp.int32)


def project_kernel(block, n, n_exp, rows, me, *refs):
    count = max(block) + n - min(block)
    pieces, (weights, *outs) = refs[:count], refs[count:]
    outs, (x, w, x_sem, w_sem) = outs[:n_exp], outs[n_exp:]
    z, expert = me[0], me[2]
    cols = weights.shape[2]
    copies = []
    for i in range(2):
        to = w.at[:, pl.ds(i * cols, cols)]
        copies.append(pltpu.make_async_copy(weights.at[i], to, w_sem.at[i]))
        copies[-1].start()
    for k in range(n_exp):
        taken = pl.ds(pl.multiple_of((expert ^ k) * rows, 16), rows)
        for i, s in enumerate(block):
            to = x.at[pl.ds((k * len(block) + i) * rows, rows)]
            copy_shard(z, n, s, pieces, taken, to, x_sem.at[k * len(block) + i], min(block))
    for c in copies:
        c.wait()
    for i in range(n_exp * len(block)):
        to = x.at[pl.ds(i * rows, rows)]
        pltpu.make_async_copy(pieces[0].at[pl.ds(0, rows)], to, x_sem.at[i]).wait()
    size = rows * len(block)
    for k in range(n_exp):
        outs[k][...] = jnp.dot(
            x[pl.ds(k * size, size), :], w[...], preferred_element_type=F32
        ).astype(BF)


def project_call(block, n, n_exp, rows, pieces, weights):
    size = rows * len(block)
    depth, cols = weights.shape[1:]
    pieces = pieces[min(block) : max(block) + n]
    flops = 4 * n_exp * size * depth * cols
    return pl.pallas_call(
        lambda *refs: project_kernel(block, n, n_exp, rows, *refs),
        name="project",
        out_shape=[jax.ShapeDtypeStruct((size, 2 * cols), BF)] * n_exp,
        in_specs=[SMEM] + [ANY] * (len(pieces) + 1),
        out_specs=[VMEM] * n_exp,
        scratch_shapes=[
            pltpu.VMEM((n_exp * size, depth), BF),
            pltpu.VMEM((depth, 2 * cols), BF),
            pltpu.SemaphoreType.DMA((n_exp * len(block),)),
            pltpu.SemaphoreType.DMA((2,)),
        ],
        compiler_params=params(32),
        cost_estimate=pl.CostEstimate(flops=flops, transcendentals=0, bytes_accessed=12 << 20),
    )(where_am_i(), *pieces, weights)


def route_kernel(n, groups, me, *refs):
    pieces, (gain, *refs) = refs[: 2 * n - 1], refs[2 * n - 1 :]
    picks, outs, (x, sem) = refs[:groups], refs[groups:-2], refs[-2:]
    part = pieces[0].shape[1]
    for s in range(n):
        copy_shard(me[0], n, s, pieces, None, x.at[:, pl.ds(s * part, part)], sem.at[s])
    for s in range(n):
        pltpu.make_async_copy(pieces[0], x.at[:, pl.ds(s * part, part)], sem.at[s]).wait()
    full = x[...].astype(F32)
    scale = lax.rsqrt(jnp.mean(full * full, axis=-1, keepdims=True) + 1e-06)
    moe_in = (full * scale * gain[...]).astype(BF)
    n_exp = len(outs) // groups
    for i in range(groups):
        for k in range(n_exp):
            outs[i * n_exp + k][...] = jnp.dot(
                picks[i][k], moe_in, preferred_element_type=F32
            ).astype(BF)


def route_call(n, pieces, gain, picks):
    n_exp, _, size = picks[0].shape
    width = n * pieces[0].shape[1]
    sizes = [p.shape[1] for p in picks for _ in range(n_exp)]
    outs = pl.pallas_call(
        lambda *refs: route_kernel(n, len(picks), *refs),
        name="route",
        out_shape=[jax.ShapeDtypeStruct((taken, width), BF) for taken in sizes],
        in_specs=[SMEM] + [ANY] * (2 * n - 1) + [VMEM] * (1 + len(picks)),
        out_specs=[VMEM] * len(sizes),
        scratch_shapes=[pltpu.VMEM((size, width), BF), pltpu.SemaphoreType.DMA((n,))],
        compiler_params=params(32),
        cost_estimate=pl.CostEstimate(
            flops=2 * sum(sizes) * size * width, transcendentals=0, bytes_accessed=12 << 20
        ),
    )(where_am_i(), *pieces, gain, *picks)
    return [outs[i : i + n_exp] for i in range(0, len(outs), n_exp)]


def gate_up_kernel(count, tiles, *refs):
    pieces, weights, (out, x, w, acc, x_sem, w_sem) = (
        refs[:count],
        refs[count : count + 2],
        refs[count + 2 :],
    )
    units, deep = weights[0].shape[1:]
    tile = deep // tiles
    each = pieces[0].shape[0]

    def copies(t):
        made = []
        for i in range(4):
            made.append(
                pltpu.make_async_copy(
                    weights[i // 2].at[i % 2, :, pl.ds(t * tile, tile)],
                    w.at[t % 2, pl.ds(i * units, units)],
                    w_sem.at[t % 2, i],
                )
            )
        return made

    moves = [
        pltpu.make_async_copy(p, x.at[pl.ds(i * each, each)], x_sem.at[i])
        for i, p in enumerate(pieces)
    ]
    for c in copies(0) + moves + copies(1):
        c.start()
    for c in moves:
        c.wait()
    for t in range(tiles):
        for c in copies(t):
            c.wait()
        product = lax.dot_general(
            x[:, pl.ds(t * tile, tile)],
            w[t % 2],
            (((1,), (1,)), ((), ())),
            preferred_element_type=F32,
        )
        acc[...] = product if t == 0 else acc[...] + product
        if t + 2 < tiles:
            for c in copies(t + 2):
                c.start()
    gate, up = acc[:, : 2 * units], acc[:, 2 * units :]
    out[...] = (gate / (1.0 + jnp.exp(-gate)) * up).astype(BF)


def gate_up_call(pieces, weights):
    units, deep = weights[0].shape[1:]
    if pieces[0].shape[0] % 16:
        pieces = [jnp.concatenate(pieces, axis=0)]
    size = len(pieces) * pieces[0].shape[0]
    tiles = 4
    return pl.pallas_call(
        lambda *refs: gate_up_kernel(len(pieces), tiles, *refs),
        name="gate_up",
        out_shape=jax.ShapeDtypeStruct((size, 2 * units), BF),
        in_specs=[ANY] * (len(pieces) + 2),
        out_specs=VMEM,
        scratch_shapes=[
            pltpu.VMEM((size, deep), BF),
            pltpu.VMEM((2, 4 * units, deep // tiles), BF),
            pltpu.VMEM((size, 4 * units), F32),
            pltpu.SemaphoreType.DMA((len(pieces),)),
            pltpu.SemaphoreType.DMA((2, 4)),
        ],
        compiler_params=params(48),
        cost_estimate=pl.CostEstimate(
            flops=8 * size * deep * units,
            transcendentals=2 * size * units,
            bytes_accessed=8 * units * deep + 2 * size * deep,
        ),
    )(*pieces, *weights)


def down_kernel(n, count, me, *refs):
    pieces, (weights, *outs) = refs[: 2 * n - 1], refs[2 * n - 1 :]
    outs, (x, w, acc, x_sem, w_sem) = outs[:count], outs[count:]
    cols = weights.shape[2]
    deep = weights.shape[1] // n

    def copies(s):
        return [
            pltpu.make_async_copy(
                weights.at[i, pl.ds(s * deep, deep)],
                w.at[s, :, pl.ds(i * cols, cols)],
                w_sem.at[s, i],
            )
            for i in range(2)
        ]

    for s in range(n):
        copy_shard(me[0], n, s, pieces, None, x.at[s], x_sem.at[s])
        for c in copies(s):
            c.start()
    for s in range(n):
        pltpu.make_async_copy(pieces[0], x.at[s], x_sem.at[s]).wait()
        for c in copies(s):
            c.wait()
        product = jnp.dot(x[s], w[s], preferred_element_type=F32)
        acc[...] = product if s == 0 else acc[...] + product
    each = acc.shape[0] // count
    for i in range(count):
        outs[i][...] = acc[pl.ds(i * each, each), :].astype(BF)


def down_call(n, n_exp, pieces, weights):
    size, deep = pieces[0].shape
    cols = weights.shape[2]
    count = n_exp if size // n_exp % 16 == 0 else 1
    outs = pl.pallas_call(
        lambda *refs: down_kernel(n, count, *refs),
        name="down",
        out_shape=[jax.ShapeDtypeStruct((size // count, 2 * cols), BF)] * count,
        in_specs=[SMEM] + [ANY] * (2 * n),
        out_specs=[VMEM] * count,
        scratch_shapes=[
            pltpu.VMEM((n, size, deep), BF),
            pltpu.VMEM((n, deep, 2 * cols), BF),
            pltpu.VMEM((size, 2 * cols), F32),
            pltpu.SemaphoreType.DMA((n,)),
            pltpu.SemaphoreType.DMA((n, 2)),
        ],
        compiler_params=params(40),
        cost_estimate=pl.CostEstimate(
            flops=4 * n * size * deep * cols, transcendentals=0, bytes_accessed=20 << 20
        ),
    )(where_am_i(), *pieces, weights)
    return outs if count == n_exp else list(outs[0].reshape(n_exp, -1, 2 * cols))


def absolute(pieces, axis):
    n = len(pieces)
    z = lax.axis_index("z")
    stacked = jnp.stack(pieces)
    return jnp.concatenate(
        [
            lax.dynamic_index_in_dim(stacked, lax.rem(z - s + n, n), 0, keepdims=False)
            for s in range(n)
        ],
        axis=axis,
    )


def attention(queries, keys, values, decay_rate, start_state, named):
    core, z, n_z = lax.axis_index("core"), lax.axis_index("z"), lax.axis_size("z")
    heads, head_dim = start_state.shape[:2]
    length = queries.shape[0]
    queries = queries.reshape(length, heads, head_dim)
    keys = keys.reshape(length, heads, head_dim)
    values = values.reshape(length, heads, head_dim)
    positions = jnp.arange(length)
    upto = positions[:, None] <= positions[None, :]
    cum = jnp.dot(decay_rate, upto.astype(F32), precision=lax.Precision.HIGHEST)
    total = cum[:, -1]
    scaled_keys = keys.astype(F32) * jnp.exp(cum - total[:, None]).T[:, :, None]
    local = jnp.einsum(
        "shd,she->hde", scaled_keys, values.astype(F32), precision=lax.Precision.HIGHEST
    )
    tall = named.shape[1]
    note = jnp.concatenate([named, total.reshape(-1, tall)], axis=0)
    notes = jnp.stack([note] + [shift_z(note, k, True) for k in range(1, n_z)])
    named, totals = notes[:, : named.shape[0]], notes[:, named.shape[0] :].reshape(n_z, heads)
    other_local = swap_core(local.astype(BF)).astype(F32)
    totals0, totals1 = by_core(core, totals, swap_core(totals))
    total0, total1 = totals0[0], totals1[0]
    half = heads // 2

    def mine(x):
        return lax.dynamic_slice_in_dim(x, core * half, half, 0)

    own_half, other_half = mine(local), mine(other_local)
    local0, local1 = by_core(core, own_half, other_half)
    chip_state = (jnp.exp(-mine(total1))[:, None, None] * local0 + local1).astype(BF)
    earlier_states = [shift_z(chip_state, k) for k in range(1, n_z)]
    earlier_totals = [
        jnp.where(z >= k, totals0[k] + totals1[k], 0.0) for k in range(1, n_z)
    ]

    causal = upto.T[None, :, :]
    diff = cum[:, None, :] - cum[:, :, None]
    decay = jnp.where(causal, jnp.exp(jnp.where(causal, diff, 0.0)), 0.0)
    scores = jnp.einsum("thd,shd->hts", queries, keys, preferred_element_type=F32)
    weights = (scores * decay).astype(BF)
    intra = jnp.einsum("hts,shd->thd", weights, values, preferred_element_type=F32)

    earlier_states = after(earlier_states, intra)
    passed = jnp.zeros_like(total)
    incoming = jnp.zeros((half, head_dim, head_dim), F32)
    for state, decayed in zip(earlier_states, earlier_totals):
        incoming = incoming + jnp.exp(-mine(passed))[:, None, None] * state.astype(F32)
        passed = passed + decayed
    incoming = incoming + jnp.exp(-mine(passed))[:, None, None] * mine(start_state)
    incoming = incoming.astype(BF)
    in0, in1 = by_core(core, incoming, swap_core(incoming))
    incoming = jnp.concatenate([in0, in1], axis=0).astype(F32)
    incoming = jnp.where(
        core == 0, incoming, jnp.exp(-total0)[:, None, None] * incoming + other_local
    )
    inter = jnp.einsum(
        "thd,hde->the", queries.astype(F32), incoming, precision=lax.Precision.HIGHEST
    )
    attended = intra + inter * jnp.exp(-cum).T[:, :, None]
    scale = lax.rsqrt(jnp.mean(attended * attended, axis=-1, keepdims=True) + 1e-06)
    return (attended * scale).astype(BF).reshape(length, heads * head_dim), list(named)


def shards(
    residual,
    attn_queries,
    attn_keys,
    attn_values,
    decay_rate,
    start_state,
    out_proj,
    moe_gain,
    gate_proj,
    up_proj,
    down_proj,
    expert_ids,
    expert_gates,
):
    n_z, n_exp = lax.axis_size("z"), lax.axis_size("expert")
    z, core, expert = lax.axis_index("z"), lax.axis_index("core"), lax.axis_index("expert")
    rows, width = residual.shape
    part = width // n_z
    capacity = 3 * rows // n_exp

    w_out, w_gate, w_up, w_down = [
        lax.all_gather(w, "core") for w in (out_proj, gate_proj[0].T, up_proj[0].T, down_proj[0])
    ]

    named = jnp.concatenate([expert_ids.astype(F32), expert_gates], axis=1)

    def columns_of(k):
        return lax.dynamic_slice_in_dim(residual, lax.rem(z + k, n_z) * part, part, axis=1)

    kept = [columns_of(0)] + [shift_z(columns_of(k), k, True) for k in range(1, n_z)]
    kept = absolute(kept, 0).reshape(n_z, rows, part)

    head_out, named = attention(
        attn_queries, attn_keys, attn_values, decay_rate, start_state, named
    )
    named = absolute([x[None] for x in named], 0)
    ids, gates = named[:, :, :2].astype(jnp.int32), named[:, :, 2:]

    partner = expert ^ jnp.arange(n_exp)
    names = ids[:, :, :, None] == partner
    member = jnp.any(names, axis=2)
    before = jnp.arange(rows)[None, :] < jnp.arange(rows)[:, None]
    slot = jnp.einsum(
        "tu,suk->stk", before.astype(BF), member.astype(BF), preferred_element_type=F32
    ).astype(jnp.int32)
    places = jnp.arange(capacity)
    placed = member[:, :, :, None] & (slot[:, :, :, None] == places)
    chosen = names[:, :, :, :, None] & (slot[:, :, None, :, None] == places)
    chosen = chosen.astype(BF).reshape(n_z, rows, 2, n_exp * capacity)

    acts, _ = line_gather(head_out)
    gain = moe_gain.reshape(1, width)

    def of_block(x, block):
        return jnp.stack([x[s] for s in block])

    def project(block, first):
        pieces = project_call(block, n_z, n_exp, rows, acts, w_out)
        arrived = [pieces[0]] + [
            to_expert(after(pieces[k], first), k) for k in range(1, n_exp)
        ]
        total = jnp.concatenate([kept[s] for s in block], axis=0).astype(F32)
        for x in arrived:
            total = total + x.astype(F32)
        return total.astype(BF), arrived

    def route(block, groups, pieces):
        picks = []
        for group in groups:
            here = jnp.array([[s == t for t in block] for s in group])[None, :, None, :, None]
            one = of_block(placed, group).transpose(2, 0, 3, 1)[:, :, :, None, :] & here
            one = one.astype(BF)
            picks.append(one.reshape(n_exp, len(group) * capacity, len(block) * rows))
        return route_call(n_z, pieces, gain, picks)

    def down(hidden):
        return down_call(n_z, n_exp, hidden, w_down)

    def combine(block, stream, expert_out):
        returned = [to_expert(expert_out[k], k) if k else expert_out[k] for k in range(n_exp)]
        returned = [x.reshape(len(block), capacity, part) for x in returned]
        returned = jnp.concatenate(returned, axis=1)
        out = stream.reshape(len(block), rows, part).astype(F32)
        for j in range(2):
            picked = jnp.einsum(
                "str,srd->std",
                of_block(chosen, block)[:, :, j],
                returned,
                preferred_element_type=F32,
            )
            out = out + picked * of_block(gates, block)[:, :, j, None]
        return out.astype(BF)

    middle_first = sorted(range(n_z), key=lambda s: abs(2 * s - n_z + 1))
    size = n_z // len(GROUPS)
    near = slice(n_z - 2, n_z + 1)
    groups, streams, waiting = [], [], []
    summed = sent = full = routed = hidden = ()
    for i, count in enumerate(GROUPS):
        block = middle_first[i * size : (i + 1) * size]
        stream, summed = project(block, summed)
        full, _ = line_gather(after(stream, full, sent))
        fine = [block[j : j + size // count] for j in range(0, size, size // count)]
        sent = route(block, fine, full)
        for group, rows_for in zip(fine, sent):
            routed = [rows_for[0]] + [
                to_expert(after(rows_for[k], routed), k) for k in range(1, n_exp)
            ]
            started = hidden[near]
            made = gate_up_call([after(x, started) for x in routed], (w_gate, w_up))
            last = i + 1 == len(GROUPS) and group is fine[-1]
            hidden, downs = line_gather(
                after(made, hidden[1:-1]), waiting if last else [], down
            )
            at = [block.index(s) * rows for s in group]
            groups.append(group)
            streams.append(jnp.stack([stream[r : r + rows] for r in at]))
            waiting.append(hidden)
    downs.append(down(hidden))
    out = [None] * n_z
    for group, stream, expert_out in zip(groups, streams, downs):
        for s, piece in zip(group, combine(group, stream, expert_out)):
            out[s] = piece
    out = jnp.stack(out)

    def rows_of(k):
        return lax.dynamic_index_in_dim(out, lax.rem(z + k, n_z), 0, keepdims=False)

    return absolute([rows_of(0)] + [shift_z(rows_of(k), k, True) for k in range(1, n_z)], 1)


def solution(mesh):
    n_ctx, n_exp = mesh.shape["context"], mesh.shape["expert"]
    fine = Mesh(mesh.devices.reshape(n_ctx // 2, 2, n_exp), ("z", "core", "expert"))
    ctx = ("z", "core")
    owner = ("z", "core", "expert")
    placed = (
        P(owner, None),
        P(ctx, "expert"),
        P(ctx, "expert"),
        P(ctx, "expert"),
        P("expert", ctx),
        P("expert", None, None),
        P("expert", ctx),
        P(),
        P("expert", None, ctx),
        P("expert", None, ctx),
        P("expert", None, ctx),
        P(owner, None),
        P(owner, None),
    )
    return jax.shard_map(
        shards, mesh=fine, in_specs=placed, out_specs=P(owner, None), check_vma=False
    )
```

```python
import jax
import jax.numpy as jnp
from jax import lax
from jax.experimental import pallas as pl
from jax.experimental.pallas import tpu as pltpu
from jax.sharding import Mesh
from jax.sharding import PartitionSpec as P

BF = jnp.bfloat16
F32 = jnp.float32
GROUPS = (2, 1)


def after(x, *first):
    return lax.optimization_barrier((x, first))[0]


def swap_core(x):
    return lax.ppermute(x, "core", [(0, 1), (1, 0)])


def shift_z(x, by, wrap=False):
    n = lax.axis_size("z")
    if wrap:
        perm = [(i, (i + by) % n) for i in range(n)]
    else:
        perm = [(i, i + by) for i in range(n) if 0 <= i + by < n]
    return lax.ppermute(x, "z", perm)


def to_expert(x, k):
    n = lax.axis_size("expert")
    return lax.ppermute(x, "expert", [(i, i ^ k) for i in range(n)])


def by_core(core, own, other):
    first = core == 0
    return jnp.where(first, own, other), jnp.where(first, other, own)


def line_gather(x, pending=(), work=None):
    n = lax.axis_size("z")
    right, left, made = [x], [x], []
    for step in range(n - 1):
        onward = [(i, i + 1) for i in range(step, n - 1)]
        held = (right[-1], left[-1])
        if made and len(made) == step:
            held, made[-1] = lax.optimization_barrier((held, made[-1]))
        elif step:
            held = lax.optimization_barrier(held)
        now = None
        if step < len(pending):
            held, now = lax.optimization_barrier((held, pending[step]))
        right.append(lax.ppermute(held[0], "z", onward))
        left.append(lax.ppermute(held[1], "z", [(n - 1 - i, n - 1 - j) for i, j in onward]))
        if now is not None:
            made.append(work(now))
    made += [work(x) for x in pending[n - 1 :]]
    return right[:0:-1] + left, made


def copy_shard(z, n, s, pieces, rows, target, sem, skipped=0):
    for i in range(s, s + n):

        @pl.when(n - 1 + s - z == i)
        def _(piece=pieces[i - skipped]):
            source = piece if rows is None else piece.at[rows]
            pltpu.make_async_copy(source, target, sem).start()


ANY = pl.BlockSpec(memory_space=pltpu.HBM)
VMEM = pl.BlockSpec(memory_space=pltpu.VMEM)
SMEM = pl.BlockSpec(memory_space=pltpu.SMEM)


def params(megabytes):
    return pltpu.CompilerParams(vmem_limit_bytes=megabytes << 20)


def where_am_i():
    return jnp.stack([lax.axis_index(a) for a in ("z", "core", "expert")]).astype(jnp.int32)


def project_kernel(block, n, n_exp, rows, me, *refs):
    count = max(block) + n - min(block)
    pieces, (weights, *outs) = refs[:count], refs[count:]
    outs, (x, w, x_sem, w_sem) = outs[:n_exp], outs[n_exp:]
    z, expert = me[0], me[2]
    cols = weights.shape[2]
    copies = []
    for i in range(2):
        to = w.at[:, pl.ds(i * cols, cols)]
        copies.append(pltpu.make_async_copy(weights.at[i], to, w_sem.at[i]))
        copies[-1].start()
    for k in range(n_exp):
        taken = pl.ds(pl.multiple_of((expert ^ k) * rows, 16), rows)
        for i, s in enumerate(block):
            to = x.at[pl.ds((k * len(block) + i) * rows, rows)]
            copy_shard(z, n, s, pieces, taken, to, x_sem.at[k * len(block) + i], min(block))
    for c in copies:
        c.wait()
    for i in range(n_exp * len(block)):
        to = x.at[pl.ds(i * rows, rows)]
        pltpu.make_async_copy(pieces[0].at[pl.ds(0, rows)], to, x_sem.at[i]).wait()
    size = rows * len(block)
    for k in range(n_exp):
        outs[k][...] = jnp.dot(
            x[pl.ds(k * size, size), :], w[...], preferred_element_type=F32
        ).astype(BF)


def project_call(block, n, n_exp, rows, pieces, weights):
    size = rows * len(block)
    depth, cols = weights.shape[1:]
    pieces = pieces[min(block) : max(block) + n]
    flops = 4 * n_exp * size * depth * cols
    return pl.pallas_call(
        lambda *refs: project_kernel(block, n, n_exp, rows, *refs),
        name="project",
        out_shape=[jax.ShapeDtypeStruct((size, 2 * cols), BF)] * n_exp,
        in_specs=[SMEM] + [ANY] * (len(pieces) + 1),
        out_specs=[VMEM] * n_exp,
        scratch_shapes=[
            pltpu.VMEM((n_exp * size, depth), BF),
            pltpu.VMEM((depth, 2 * cols), BF),
            pltpu.SemaphoreType.DMA((n_exp * len(block),)),
            pltpu.SemaphoreType.DMA((2,)),
        ],
        compiler_params=params(32),
        cost_estimate=pl.CostEstimate(flops=flops, transcendentals=0, bytes_accessed=12 << 20),
    )(where_am_i(), *pieces, weights)


def route_kernel(n, groups, me, *refs):
    pieces, (gain, *refs) = refs[: 2 * n - 1], refs[2 * n - 1 :]
    picks, outs, (x, sem) = refs[:groups], refs[groups:-2], refs[-2:]
    part = pieces[0].shape[1]
    for s in range(n):
        copy_shard(me[0], n, s, pieces, None, x.at[:, pl.ds(s * part, part)], sem.at[s])
    for s in range(n):
        pltpu.make_async_copy(pieces[0], x.at[:, pl.ds(s * part, part)], sem.at[s]).wait()
    full = x[...].astype(F32)
    scale = lax.rsqrt(jnp.mean(full * full, axis=-1, keepdims=True) + 1e-06)
    moe_in = (full * scale * gain[...]).astype(BF)
    n_exp = len(outs) // groups
    for i in range(groups):
        for k in range(n_exp):
            outs[i * n_exp + k][...] = jnp.dot(
                picks[i][k], moe_in, preferred_element_type=F32
            ).astype(BF)


def route_call(n, pieces, gain, picks):
    n_exp, _, size = picks[0].shape
    width = n * pieces[0].shape[1]
    sizes = [p.shape[1] for p in picks for _ in range(n_exp)]
    outs = pl.pallas_call(
        lambda *refs: route_kernel(n, len(picks), *refs),
        name="route",
        out_shape=[jax.ShapeDtypeStruct((taken, width), BF) for taken in sizes],
        in_specs=[SMEM] + [ANY] * (2 * n - 1) + [VMEM] * (1 + len(picks)),
        out_specs=[VMEM] * len(sizes),
        scratch_shapes=[pltpu.VMEM((size, width), BF), pltpu.SemaphoreType.DMA((n,))],
        compiler_params=params(32),
        cost_estimate=pl.CostEstimate(
            flops=2 * sum(sizes) * size * width, transcendentals=0, bytes_accessed=12 << 20
        ),
    )(where_am_i(), *pieces, gain, *picks)
    return [outs[i : i + n_exp] for i in range(0, len(outs), n_exp)]


def gate_up_kernel(count, tiles, *refs):
    pieces, weights, (out, x, w, acc, x_sem, w_sem) = (
        refs[:count],
        refs[count : count + 2],
        refs[count + 2 :],
    )
    units, deep = weights[0].shape[1:]
    tile = deep // tiles
    each = pieces[0].shape[0]

    def copies(t):
        made = []
        for i in range(4):
            made.append(
                pltpu.make_async_copy(
                    weights[i // 2].at[i % 2, :, pl.ds(t * tile, tile)],
                    w.at[t % 2, pl.ds(i * units, units)],
                    w_sem.at[t % 2, i],
                )
            )
        return made

    moves = [
        pltpu.make_async_copy(p, x.at[pl.ds(i * each, each)], x_sem.at[i])
        for i, p in enumerate(pieces)
    ]
    for c in copies(0) + moves + copies(1):
        c.start()
    for c in moves:
        c.wait()
    for t in range(tiles):
        for c in copies(t):
            c.wait()
        product = lax.dot_general(
            x[:, pl.ds(t * tile, tile)],
            w[t % 2],
            (((1,), (1,)), ((), ())),
            preferred_element_type=F32,
        )
        acc[...] = product if t == 0 else acc[...] + product
        if t + 2 < tiles:
            for c in copies(t + 2):
                c.start()
    gate, up = acc[:, : 2 * units], acc[:, 2 * units :]
    out[...] = (gate / (1.0 + jnp.exp(-gate)) * up).astype(BF)


def gate_up_call(pieces, weights):
    units, deep = weights[0].shape[1:]
    if pieces[0].shape[0] % 16:
        pieces = [jnp.concatenate(pieces, axis=0)]
    size = len(pieces) * pieces[0].shape[0]
    tiles = 4
    return pl.pallas_call(
        lambda *refs: gate_up_kernel(len(pieces), tiles, *refs),
        name="gate_up",
        out_shape=jax.ShapeDtypeStruct((size, 2 * units), BF),
        in_specs=[ANY] * (len(pieces) + 2),
        out_specs=VMEM,
        scratch_shapes=[
            pltpu.VMEM((size, deep), BF),
            pltpu.VMEM((2, 4 * units, deep // tiles), BF),
            pltpu.VMEM((size, 4 * units), F32),
            pltpu.SemaphoreType.DMA((len(pieces),)),
            pltpu.SemaphoreType.DMA((2, 4)),
        ],
        compiler_params=params(48),
        cost_estimate=pl.CostEstimate(
            flops=8 * size * deep * units,
            transcendentals=2 * size * units,
            bytes_accessed=8 * units * deep + 2 * size * deep,
        ),
    )(*pieces, *weights)


def down_kernel(n, count, me, *refs):
    pieces, (weights, *outs) = refs[: 2 * n - 1], refs[2 * n - 1 :]
    outs, (x, w, acc, x_sem, w_sem) = outs[:count], outs[count:]
    cols = weights.shape[2]
    deep = weights.shape[1] // n

    def copies(s):
        return [
            pltpu.make_async_copy(
                weights.at[i, pl.ds(s * deep, deep)],
                w.at[s, :, pl.ds(i * cols, cols)],
                w_sem.at[s, i],
            )
            for i in range(2)
        ]

    for s in range(n):
        copy_shard(me[0], n, s, pieces, None, x.at[s], x_sem.at[s])
        for c in copies(s):
            c.start()
    for s in range(n):
        pltpu.make_async_copy(pieces[0], x.at[s], x_sem.at[s]).wait()
        for c in copies(s):
            c.wait()
        product = jnp.dot(x[s], w[s], preferred_element_type=F32)
        acc[...] = product if s == 0 else acc[...] + product
    each = acc.shape[0] // count
    for i in range(count):
        outs[i][...] = acc[pl.ds(i * each, each), :].astype(BF)


def down_call(n, n_exp, pieces, weights):
    size, deep = pieces[0].shape
    cols = weights.shape[2]
    count = n_exp if size // n_exp % 16 == 0 else 1
    outs = pl.pallas_call(
        lambda *refs: down_kernel(n, count, *refs),
        name="down",
        out_shape=[jax.ShapeDtypeStruct((size // count, 2 * cols), BF)] * count,
        in_specs=[SMEM] + [ANY] * (2 * n),
        out_specs=[VMEM] * count,
        scratch_shapes=[
            pltpu.VMEM((n, size, deep), BF),
            pltpu.VMEM((n, deep, 2 * cols), BF),
            pltpu.VMEM((size, 2 * cols), F32),
            pltpu.SemaphoreType.DMA((n,)),
            pltpu.SemaphoreType.DMA((n, 2)),
        ],
        compiler_params=params(40),
        cost_estimate=pl.CostEstimate(
            flops=4 * n * size * deep * cols, transcendentals=0, bytes_accessed=20 << 20
        ),
    )(where_am_i(), *pieces, weights)
    return outs if count == n_exp else list(outs[0].reshape(n_exp, -1, 2 * cols))


def absolute(pieces, axis):
    n = len(pieces)
    z = lax.axis_index("z")
    stacked = jnp.stack(pieces)
    return jnp.concatenate(
        [
            lax.dynamic_index_in_dim(stacked, lax.rem(z - s + n, n), 0, keepdims=False)
            for s in range(n)
        ],
        axis=axis,
    )


def attention(queries, keys, values, decay_rate, start_state, named):
    core, z, n_z = lax.axis_index("core"), lax.axis_index("z"), lax.axis_size("z")
    heads, head_dim = start_state.shape[:2]
    length = queries.shape[0]
    queries = queries.reshape(length, heads, head_dim)
    keys = keys.reshape(length, heads, head_dim)
    values = values.reshape(length, heads, head_dim)
    positions = jnp.arange(length)
    upto = positions[:, None] <= positions[None, :]
    cum = jnp.dot(decay_rate, upto.astype(F32), precision=lax.Precision.HIGHEST)
    total = cum[:, -1]
    scaled_keys = keys.astype(F32) * jnp.exp(cum - total[:, None]).T[:, :, None]
    local = jnp.einsum(
        "shd,she->hde", scaled_keys, values.astype(F32), precision=lax.Precision.HIGHEST
    )
    tall = named.shape[1]
    note = jnp.concatenate([named, total.reshape(-1, tall)], axis=0)
    notes = jnp.stack([note] + [shift_z(note, k, True) for k in range(1, n_z)])
    named, totals = notes[:, : named.shape[0]], notes[:, named.shape[0] :].reshape(n_z, heads)
    other_local = swap_core(local.astype(BF)).astype(F32)
    totals0, totals1 = by_core(core, totals, swap_core(totals))
    total0, total1 = totals0[0], totals1[0]
    half = heads // 2

    def mine(x):
        return lax.dynamic_slice_in_dim(x, core * half, half, 0)

    own_half, other_half = mine(local), mine(other_local)
    local0, local1 = by_core(core, own_half, other_half)
    chip_state = (jnp.exp(-mine(total1))[:, None, None] * local0 + local1).astype(BF)
    earlier_states = [shift_z(chip_state, k) for k in range(1, n_z)]
    earlier_totals = [
        jnp.where(z >= k, totals0[k] + totals1[k], 0.0) for k in range(1, n_z)
    ]

    causal = upto.T[None, :, :]
    diff = cum[:, None, :] - cum[:, :, None]
    decay = jnp.where(causal, jnp.exp(jnp.where(causal, diff, 0.0)), 0.0)
    scores = jnp.einsum("thd,shd->hts", queries, keys, preferred_element_type=F32)
    weights = (scores * decay).astype(BF)
    intra = jnp.einsum("hts,shd->thd", weights, values, preferred_element_type=F32)

    earlier_states = after(earlier_states, intra)
    passed = jnp.zeros_like(total)
    incoming = jnp.zeros((half, head_dim, head_dim), F32)
    for state, decayed in zip(earlier_states, earlier_totals):
        incoming = incoming + jnp.exp(-mine(passed))[:, None, None] * state.astype(F32)
        passed = passed + decayed
    incoming = incoming + jnp.exp(-mine(passed))[:, None, None] * mine(start_state)
    incoming = incoming.astype(BF)
    in0, in1 = by_core(core, incoming, swap_core(incoming))
    incoming = jnp.concatenate([in0, in1], axis=0).astype(F32)
    incoming = jnp.where(
        core == 0, incoming, jnp.exp(-total0)[:, None, None] * incoming + other_local
    )
    inter = jnp.einsum(
        "thd,hde->the", queries.astype(F32), incoming, precision=lax.Precision.HIGHEST
    )
    attended = intra + inter * jnp.exp(-cum).T[:, :, None]
    scale = lax.rsqrt(jnp.mean(attended * attended, axis=-1, keepdims=True) + 1e-06)
    return (attended * scale).astype(BF).reshape(length, heads * head_dim), list(named)


def shards(
    residual,
    attn_queries,
    attn_keys,
    attn_values,
    decay_rate,
    start_state,
    out_proj,
    moe_gain,
    gate_proj,
    up_proj,
    down_proj,
    expert_ids,
    expert_gates,
):
    n_z, n_exp = lax.axis_size("z"), lax.axis_size("expert")
    z, core, expert = lax.axis_index("z"), lax.axis_index("core"), lax.axis_index("expert")
    rows, width = residual.shape
    part = width // n_z
    capacity = 3 * rows // n_exp

    w_out, w_gate, w_up, w_down = [
        lax.all_gather(w, "core") for w in (out_proj, gate_proj[0].T, up_proj[0].T, down_proj[0])
    ]

    named = jnp.concatenate([expert_ids.astype(F32), expert_gates], axis=1)

    def columns_of(k):
        return lax.dynamic_slice_in_dim(residual, lax.rem(z + k, n_z) * part, part, axis=1)

    kept = [columns_of(0)] + [shift_z(columns_of(k), k, True) for k in range(1, n_z)]
    kept = absolute(kept, 0).reshape(n_z, rows, part)

    head_out, named = attention(
        attn_queries, attn_keys, attn_values, decay_rate, start_state, named
    )
    named = absolute([x[None] for x in named], 0)
    ids, gates = named[:, :, :2].astype(jnp.int32), named[:, :, 2:]

    partner = expert ^ jnp.arange(n_exp)
    names = ids[:, :, :, None] == partner
    member = jnp.any(names, axis=2)
    before = jnp.arange(rows)[None, :] < jnp.arange(rows)[:, None]
    slot = jnp.einsum(
        "tu,suk->stk", before.astype(BF), member.astype(BF), preferred_element_type=F32
    ).astype(jnp.int32)
    places = jnp.arange(capacity)
    placed = member[:, :, :, None] & (slot[:, :, :, None] == places)
    chosen = names[:, :, :, :, None] & (slot[:, :, None, :, None] == places)
    chosen = chosen.astype(BF).reshape(n_z, rows, 2, n_exp * capacity)

    acts, _ = line_gather(head_out)
    gain = moe_gain.reshape(1, width)

    def of_block(x, block):
        return jnp.stack([x[s] for s in block])

    def project(block, first):
        pieces = project_call(block, n_z, n_exp, rows, acts, w_out)
        arrived = [pieces[0]] + [
            to_expert(pieces[k], k) for k in range(1, n_exp)
        ]
        total = jnp.concatenate([kept[s] for s in block], axis=0).astype(F32)
        for x in arrived:
            total = total + x.astype(F32)
        return total.astype(BF), arrived

    def route(block, groups, pieces):
        picks = []
        for group in groups:
            here = jnp.array([[s == t for t in block] for s in group])[None, :, None, :, None]
            one = of_block(placed, group).transpose(2, 0, 3, 1)[:, :, :, None, :] & here
            one = one.astype(BF)
            picks.append(one.reshape(n_exp, len(group) * capacity, len(block) * rows))
        return route_call(n_z, pieces, gain, picks)

    def down(hidden):
        return down_call(n_z, n_exp, hidden, w_down)

    def combine(block, stream, expert_out):
        returned = [to_expert(expert_out[k], k) if k else expert_out[k] for k in range(n_exp)]
        returned = [x.reshape(len(block), capacity, part) for x in returned]
        returned = jnp.concatenate(returned, axis=1)
        out = stream.reshape(len(block), rows, part).astype(F32)
        for j in range(2):
            picked = jnp.einsum(
                "str,srd->std",
                of_block(chosen, block)[:, :, j],
                returned,
                preferred_element_type=F32,
            )
            out = out + picked * of_block(gates, block)[:, :, j, None]
        return out.astype(BF)

    middle_first = sorted(range(n_z), key=lambda s: abs(2 * s - n_z + 1))
    size = n_z // len(GROUPS)
    near = slice(n_z - 2, n_z + 1)
    groups, streams, waiting = [], [], []
    summed = sent = full = routed = hidden = ()
    for i, count in enumerate(GROUPS):
        block = middle_first[i * size : (i + 1) * size]
        stream, summed = project(block, summed)
        full, _ = line_gather(after(stream, full, sent))
        fine = [block[j : j + size // count] for j in range(0, size, size // count)]
        sent = route(block, fine, full)
        for group, rows_for in zip(fine, sent):
            routed = [rows_for[0]] + [
                to_expert(after(rows_for[k], routed), k) for k in range(1, n_exp)
            ]
            started = hidden[near]
            made = gate_up_call([after(x, started) for x in routed], (w_gate, w_up))
            last = i + 1 == len(GROUPS) and group is fine[-1]
            hidden, downs = line_gather(
                after(made, hidden[1:-1]), waiting if last else [], down
            )
            at = [block.index(s) * rows for s in group]
            groups.append(group)
            streams.append(jnp.stack([stream[r : r + rows] for r in at]))
            waiting.append(hidden)
    downs.append(down(hidden))
    out = [None] * n_z
    for group, stream, expert_out in zip(groups, streams, downs):
        for s, piece in zip(group, combine(group, stream, expert_out)):
            out[s] = piece
    out = jnp.stack(out)

    def rows_of(k):
        return lax.dynamic_index_in_dim(out, lax.rem(z + k, n_z), 0, keepdims=False)

    return absolute([rows_of(0)] + [shift_z(rows_of(k), k, True) for k in range(1, n_z)], 1)


def solution(mesh):
    n_ctx, n_exp = mesh.shape["context"], mesh.shape["expert"]
    fine = Mesh(mesh.devices.reshape(n_ctx // 2, 2, n_exp), ("z", "core", "expert"))
    ctx = ("z", "core")
    owner = ("z", "core", "expert")
    placed = (
        P(owner, None),
        P(ctx, "expert"),
        P(ctx, "expert"),
        P(ctx, "expert"),
        P("expert", ctx),
        P("expert", None, None),
        P("expert", ctx),
        P(),
        P("expert", None, ctx),
        P("expert", None, ctx),
        P("expert", None, ctx),
        P(owner, None),
        P(owner, None),
    )
    return jax.shard_map(
        shards, mesh=fine, in_specs=placed, out_specs=P(owner, None), check_vma=False
    )
```
